128 devices in a mesh: pb: 16 (over x, z_hi, core), ka: 8 (over y, z_lo).
Axes of the slice: x: 4, y: 4, z: 4 (z_hi: 2, z_lo: 2; z = z_hi * 2 + z_lo), core: 2. Of those that a mesh axis runs over, the one named last changes fastest.
Arguments:
- atoms: bfloat16 [49152, 128], P('pb'), may hold values from -6 to 6
- atom_gain: float32 [128], replicated, may hold values from 0.1 to 1.9
- atom_qkv: bfloat16 [128, 384], replicated, may hold values from -0.5 to 0.5
- atom_proj: bfloat16 [128, 128], replicated, may hold values from -0.5 to 0.5
- atom_bias: bfloat16 [4, 49152, 128], P(None, 'pb'), may hold values from -4 to 250
- window_shift: int32 [1536], P('pb'), may hold values from -64 to -32, as said below
- token_of_atom: int32 [49152], P('pb'), may hold values from 0 to 6143, as said below
- agg_weight: bfloat16 [128, 768], replicated, may hold values from -0.5 to 0.5
- token_gain: float32 [768], replicated, may hold values from 0.1 to 1.9
- token_q: bfloat16 [768, 768], replicated, may hold values from -0.21875 to 0.21875
- token_kv: bfloat16 [768, 1536], replicated, may hold values from -0.21875 to 0.21875
- token_o: bfloat16 [768, 768], replicated, may hold values from -0.21875 to 0.21875
- pair_bias: bfloat16 [16, 6144, 6144], P(None, 'pb', 'ka'), may hold values from -4 to 250
Outputs:
- atom_out: bfloat16 [49152, 128], P('pb')
- tokens_out: bfloat16 [6144, 768], P('pb')
The draws below stay inside these ranges and needn't reach their ends.
Inputs may be any that keep to these rules, and one draw needn't show every extreme that they name: token_of_atom never falls along the atoms and names every token at least once. Of the 3072 atoms of one index of pb, all but its last ones belong to that index's own 384 tokens; for every index but the final one, its last 192 to 384 atoms belong to the tokens of the index after, and the final index's atoms are all its own. In every draw some index has all of its last 384 atoms in the index after. The key window of query block b begins at atom 32 b + window_shift[b]; both ends of the range occur in every draw.
All inputs are finite; a program needn't handle non-finite values.
Results may differ from the reference program's by a relative error of at most 0.0095.
Values may be sent and summed in bfloat16 or wider, within the bound.
A program may use at most 128 MiB of HBM per device.

```python
import math
import jax
import jax.numpy as jnp
from jax import lax

CA = 128
AH = 4
CT = 768
TH = 16
WIN_Q = 32
WIN_K = 128
TOK_DEV = 384
ATOM_DEV = 3072
SHIFT_MAX = 384
TOKENS = 6144
ATOMS = 49152
KEY_DEV = 768
N_KA = 8


def token_starts(key):
    shards = TOKENS // TOK_DEV
    key_drift, key_order, key_weight = jax.random.split(jax.random.fold_in(key, 11), 3)
    drift = jax.random.randint(key_drift, (shards + 1,), -SHIFT_MAX, -(SHIFT_MAX // 2) + 1, dtype=jnp.int32)
    order = jax.random.permutation(key_order, shards - 1) + 1
    drift = drift.at[order[0]].set(-SHIFT_MAX)
    drift = drift.at[0].set(0).at[shards].set(0)
    borders = jnp.arange(shards + 1, dtype=jnp.int32) * ATOM_DEV + drift
    surplus = borders[1:] - borders[:-1] - TOK_DEV
    weights = jax.random.randint(key_weight, (shards, TOK_DEV), 1, 33, dtype=jnp.int32)
    before = jnp.cumsum(weights, axis=1) - weights
    totals = jnp.sum(weights, axis=1)
    starts = borders[:-1, None] + jnp.arange(TOK_DEV, dtype=jnp.int32)[None, :] + before * surplus[:, None] // totals[:, None]
    return starts.reshape(-1)


def draw_token_of_atom(key, part):
    starts = token_starts(key)
    atom_index = jnp.arange(ATOMS, dtype=jnp.int32)
    return (jnp.searchsorted(starts, atom_index, side='right') - 1).astype(jnp.int32)


def draw_window_shift(key, part):
    windows = ATOMS // WIN_Q
    key_value, key_order = jax.random.split(jax.random.fold_in(key, 23), 2)
    shifts = jax.random.randint(key_value, (windows,), -(WIN_K // 2), WIN_Q - WIN_K // 2 + 1, dtype=jnp.int32)
    order = jax.random.permutation(key_order, windows)
    shifts = shifts.at[order[0]].set(-(WIN_K // 2)).at[order[1]].set(WIN_Q - WIN_K // 2)
    return shifts


def spiky_bias(key, shape):
    key_base = jax.random.fold_in(key, 0)
    base = jax.random.truncated_normal(key_base, -4.0, 4.0, shape, jnp.float32)
    return base.astype(jnp.bfloat16)


def draw_atom_bias(key, part):
    return spiky_bias(jax.random.fold_in(key, 31), (AH, ATOMS, WIN_K))


def draw_pair_bias(key, part):
    return spiky_bias(jax.random.fold_in(key, 47), (TH, TOKENS, TOKENS))


def block_levels(key, extent, pieces, smallest, top_value):
    loudness, own = 1.0, jax.random.fold_in(key, 6)
    for position, shards_of in pieces:
        heights = jnp.exp(jax.random.uniform(jax.random.fold_in(own, position), (shards_of,), jnp.float32, smallest / len(pieces), top_value / len(pieces)))
        loudness = loudness * jnp.repeat(heights, extent[position] // shards_of).reshape([-1 if axis == position else 1 for axis in range(len(extent))])
    return loudness


def noise(own_key, extent, deviation, bound, cuts=(), kind=jnp.bfloat16):
    loudness = block_levels(own_key, extent, cuts, -0.22, 0.18) if cuts else 1.0
    result = jax.random.normal(own_key, extent, jnp.float32) * deviation * loudness
    return jnp.minimum(jnp.maximum(result, -bound), bound).astype(kind)


def setup_inputs(seed: int = 0) -> dict:
    keys = jax.random.split(jax.random.key(seed), 14)
    return {
        "atoms": noise(keys[0], (ATOMS, CA), 1.0, 6.0, ((0, 16),)),
        "atom_gain": jnp.clip(1.0 + 0.18 * jax.random.normal(keys[1], (CA,), jnp.float32), 0.1, 1.9),
        "atom_qkv": noise(keys[2], (CA, 3 * CA), CA ** -0.5, 0.5),
        "atom_proj": noise(keys[3], (CA, CA), CA ** -0.5, 0.5),
        "atom_bias": draw_atom_bias(jax.random.fold_in(keys[13], 71), 0),
        "window_shift": draw_window_shift(jax.random.fold_in(keys[13], 71), 0),
        "token_of_atom": draw_token_of_atom(jax.random.fold_in(keys[13], 71), 0),
        "agg_weight": noise(keys[7], (CA, CT), CA ** -0.5, 0.5),
        "token_gain": jnp.clip(1.0 + 0.18 * jax.random.normal(keys[8], (CT,), jnp.float32), 0.1, 1.9),
        "token_q": noise(keys[9], (CT, CT), CT ** -0.5, 0.21875),
        "token_kv": noise(keys[10], (CT, 2 * CT), CT ** -0.5, 0.21875),
        "token_o": noise(keys[11], (CT, CT), CT ** -0.5, 0.21875),
        "pair_bias": draw_pair_bias(jax.random.fold_in(keys[13], 71), 0),
    }


def layer_norm(values, gain_vec):
    as_float = values.astype(jnp.float32)
    centre = lax.optimization_barrier(jnp.mean(as_float, axis=-1, keepdims=True))
    spread = lax.optimization_barrier(jnp.mean(jnp.square(as_float - centre), axis=-1, keepdims=True))
    return (as_float - centre) * lax.rsqrt(spread + 1e-05) * gain_vec

def reference(atoms, atom_gain, atom_qkv, atom_proj, atom_bias, window_shift, token_of_atom, agg_weight, token_gain, token_q, token_kv, token_o, pair_bias):
    atom_head = CA // AH
    half_win = WIN_K // 2
    normed = layer_norm(atoms, atom_gain).astype(jnp.bfloat16)
    projected = jnp.dot(normed, atom_qkv, preferred_element_type=jnp.float32).astype(jnp.bfloat16)
    blocks = ATOMS // WIN_Q
    padded = jnp.pad(projected[:, CA:], ((half_win, half_win), (0, 0)))
    window_first = jnp.arange(blocks, dtype=jnp.int32) * WIN_Q + window_shift.astype(jnp.int32)
    key_index = window_first[:, None] + jnp.arange(WIN_K, dtype=jnp.int32)[None, :]
    gathered = padded[key_index + half_win]
    in_range = (key_index >= 0) & (key_index < ATOMS)
    query_heads = projected[:, :CA].reshape(blocks, WIN_Q, AH, atom_head).astype(jnp.float32)
    key_heads = gathered[:, :, :CA].reshape(blocks, WIN_K, AH, atom_head).astype(jnp.float32)
    value_heads = gathered[:, :, CA:].reshape(blocks, WIN_K, AH, atom_head).astype(jnp.float32)
    scores = jnp.einsum('bqhd,bkhd->hbqk', query_heads, key_heads) / math.sqrt(atom_head)
    scores = scores + atom_bias.astype(jnp.float32).reshape(AH, blocks, WIN_Q, WIN_K)
    scores = jnp.where(in_range[None, :, None, :], scores, -jnp.inf)
    exp_terms = jnp.exp(scores - lax.optimization_barrier(jnp.max(scores, axis=-1, keepdims=True)))
    weights = (exp_terms / lax.optimization_barrier(jnp.sum(exp_terms, axis=-1, keepdims=True))).astype(jnp.bfloat16)
    atom_mixed = jnp.einsum('hbqk,bkhd->bqhd', weights.astype(jnp.float32), value_heads)
    atom_mixed = atom_mixed.reshape(ATOMS, CA).astype(jnp.bfloat16)
    atom_out = (atoms.astype(jnp.float32) + jnp.dot(atom_mixed, atom_proj, preferred_element_type=jnp.float32)).astype(jnp.bfloat16)
    hidden = jax.nn.silu(jnp.dot(atom_out, agg_weight, preferred_element_type=jnp.float32)).astype(jnp.bfloat16)
    token_sums = jax.ops.segment_sum(hidden.astype(jnp.float32), token_of_atom, num_segments=TOKENS)
    token_counts = jax.ops.segment_sum(jnp.ones((ATOMS,), jnp.float32), token_of_atom, num_segments=TOKENS)
    token_repr = (token_sums / token_counts[:, None]).astype(jnp.bfloat16)
    token_normed = layer_norm(token_repr, token_gain).astype(jnp.bfloat16)
    queries = jnp.dot(token_normed, token_q, preferred_element_type=jnp.float32).astype(jnp.bfloat16)
    keyvals = jnp.dot(token_normed, token_kv, preferred_element_type=jnp.float32).astype(jnp.bfloat16)
    token_head = CT // TH
    key_blocks = keyvals[:, :CT].reshape(N_KA, KEY_DEV, TH, token_head).astype(jnp.float32)
    value_blocks = keyvals[:, CT:].reshape(N_KA, KEY_DEV, TH, token_head).astype(jnp.float32)
    block_rows = math.gcd(TOKENS, 512)

    def one_block(first_row):
        query_rows = lax.dynamic_slice_in_dim(queries, first_row, block_rows, 0)
        query_rows = query_rows.reshape(block_rows, TH, token_head).astype(jnp.float32)
        bias_rows = lax.dynamic_slice_in_dim(pair_bias, first_row, block_rows, 1).astype(jnp.float32)
        bias_rows = bias_rows.reshape(TH, block_rows, N_KA, KEY_DEV)
        block_scores = jnp.einsum('qhd,nkhd->hqnk', query_rows, key_blocks) / math.sqrt(token_head) + bias_rows
        block_max = lax.optimization_barrier(jnp.max(block_scores, axis=-1, keepdims=True))
        block_exp = jnp.exp(block_scores - block_max)
        rounded = block_exp.astype(jnp.bfloat16).astype(jnp.float32)
        block_mix = jnp.einsum('hqnk,nkhd->hqnd', rounded, value_blocks)
        block_totals = lax.optimization_barrier(jnp.sum(block_exp, axis=-1))
        block_top = block_max[..., 0]
        row_max = lax.optimization_barrier(jnp.max(block_top, axis=-1, keepdims=True))
        factor = jnp.exp(block_top - row_max)
        mixed_sum = lax.optimization_barrier(jnp.sum(block_mix * factor[..., None], axis=2))
        total_sum = lax.optimization_barrier(jnp.sum(block_totals * factor, axis=-1))
        token_mixed = mixed_sum / total_sum[..., None]
        return token_mixed.transpose(1, 0, 2).reshape(block_rows, CT).astype(jnp.bfloat16)
    first_rows = jnp.arange(TOKENS // block_rows, dtype=jnp.int32) * block_rows
    token_mix = lax.map(one_block, first_rows).reshape(TOKENS, CT)
    tokens_out = (token_repr.astype(jnp.float32) + jnp.dot(token_mix, token_o, preferred_element_type=jnp.float32)).astype(jnp.bfloat16)
    return (atom_out, tokens_out)
```

```python
import functools
import math

import jax
import jax.numpy as jnp
from jax import lax
from jax.experimental import pallas as pl
from jax.experimental.pallas import tpu as pltpu
from jax.sharding import PartitionSpec as P

F32, BF16, I32 = jnp.float32, jnp.bfloat16, jnp.int32
AR, HALO, TAIL, WQ, WK = 3072, 64, 384, 32, 128
EXT = AR + 2 * HALO
TR, CT, TH, HD = 384, 768, 16, 48
PIECE = TR // 8
WINDOWS = AR // WQ
UNROLL = 4
CHUNKS = ((0, 6, 0), (6, 11, 256), (11, 16, 512))
NT = (((1,), (1,)), ((), ()))
NN = (((1,), (0,)), ((), ()))


def iota(shape, dim):
    return lax.broadcasted_iota(I32, shape, dim)


def mm(a, b, dims=NN):
    return lax.dot_general(a, b, dims, preferred_element_type=F32)


def normed(x, gain):
    centre = jnp.mean(x, axis=-1, keepdims=True)
    diff = x - centre
    spread = jnp.mean(diff * diff, axis=-1, keepdims=True)
    return (diff * lax.rsqrt(spread + 1e-05) * gain).astype(BF16)


def kernel(
    shift_ref,
    atoms_h,
    again_h,
    qkv_h,
    proj_h,
    abias_h,
    ids_h,
    agg_h,
    tgain_h,
    wq_h,
    wkv_h,
    wo_h,
    pair_h,
    aout_h,
    tout_h,
    xs,
    again,
    wqkv,
    wproj,
    ab,
    ids,
    wagg,
    tgain,
    wq,
    wkv,
    wo,
    pbm,
    qs,
    kf,
    vf,
    ms,
    ao,
    acc,
    rep,
    nrm,
    qt,
    kt,
    kk,
    vv,
    osc,
    mlb,
    mixb,
    rbuf,
    rml,
    obuf,
    lsem,
    psem,
    osem,
    hs,
    hr,
    xsem,
    xrsem,
    fs,
    fr,
    rs,
    rr,
    gs,
    gr,
):
    p = lax.axis_index("pb")
    k = lax.axis_index("ka")
    c = lax.rem(p, 2)
    cp = lax.div(p, 2)
    last = 15
    barrier = pltpu.get_barrier_semaphore()

    def dev(pb, ka):
        return {"pb": pb, "ka": ka}

    def hello(pb, ka):
        pl.semaphore_signal(barrier, inc=1, device_id=dev(pb, ka), device_id_type=pl.DeviceIdType.MESH)

    def send(src, dst, ssem, rsem, pb, ka):
        return pltpu.make_async_remote_copy(
            src_ref=src,
            dst_ref=dst,
            send_sem=ssem,
            recv_sem=rsem,
            device_id=dev(pb, ka),
            device_id_type=pl.DeviceIdType.MESH,
        )

    @pl.when(p > 0)
    def _():
        hello(p - 1, k)

    @pl.when(p < last)
    def _():
        hello(p + 1, k)

    for i in range(1, 8):
        hello(lax.rem(cp + i, 8) * 2 + c, cp)
        hello(p, lax.rem(k + i, 8))

    @pl.when(k != cp)
    def _():
        for s in range(8):
            hello(2 * k + c, s)

    copies = {}

    def load(name, src, dst, sem):
        copies[name] = pltpu.make_async_copy(src, dst, sem)
        copies[name].start()

    load("atoms", atoms_h, xs.at[pl.ds(HALO, AR)], lsem.at[0])
    load("again", again_h, again, lsem.at[1])
    load("qkv", qkv_h, wqkv, lsem.at[2])
    load("abias", abias_h, ab, lsem.at[3])
    load("proj", proj_h, wproj, lsem.at[4])
    load("agg", agg_h, wagg, lsem.at[5])
    load("ids", ids_h, ids.at[:, pl.ds(0, AR)], lsem.at[6])
    load("tgain", tgain_h, tgain, lsem.at[7])
    load("wq", wq_h, wq, lsem.at[8])
    load("wkv", wkv_h, wkv, lsem.at[9])
    load("wo", wo_h, wo, lsem.at[10])
    load("pair", pair_h, pbm, psem)

    def project(row, rows, queries):
        x = xs[pl.ds(row, rows), :].astype(F32)
        n = normed(x, again[...])
        y = mm(n, wqkv[...])
        if queries:
            qs[pl.ds(row - HALO, rows), :] = y[:, 0:128].astype(BF16)
        kf[pl.ds(row, rows), :] = y[:, 128:256].astype(BF16).astype(F32)
        vf[pl.ds(row, rows), :] = y[:, 256:384].astype(BF16).astype(F32)

    copies["atoms"].wait()
    copies["again"].wait()
    copies["qkv"].wait()

    def project_own(i, carry):
        project(pl.multiple_of(HALO + i * 384, 64), 384, True)
        return carry

    lax.fori_loop(0, AR // 384, project_own, 0)

    greeted = 14 + jnp.where(p > 0, 1, 0) + jnp.where(p < last, 1, 0) + jnp.where(k != cp, 8, 0)
    pl.semaphore_wait(barrier, greeted)

    right = jnp.minimum(p + 1, last)
    left = jnp.maximum(p - 1, 0)
    to_right = send(
        atoms_h.at[pl.ds(AR - HALO, HALO)], xs.at[pl.ds(0, HALO)], hs.at[0], hr.at[0], right, k
    )
    to_left = send(
        atoms_h.at[pl.ds(0, HALO)], xs.at[pl.ds(HALO + AR, HALO)], hs.at[1], hr.at[1], left, k
    )
    ids_right = send(
        ids_h.at[:, pl.ds(AR - TAIL, TAIL)], ids.at[:, pl.ds(AR, TAIL)], hs.at[2], hr.at[2], right, k
    )
    tail_right = send(
        ao.at[pl.ds(AR - TAIL, TAIL)], ao.at[pl.ds(AR, TAIL)], hs.at[3], hr.at[3], right, k
    )

    @pl.when(p < last)
    def _():
        to_right.start()
        ids_right.start()

    @pl.when(p > 0)
    def _():
        to_left.start()

    copies["abias"].wait()
    copies["proj"].wait()

    head_mask = jnp.where(
        (iota((128, 128), 0) >> 5) == (iota((128, 128), 1) >> 5), 1.0, 0.0
    ).astype(BF16)
    lane_head = iota((WQ, 128), 1) >> 5
    ones = jnp.ones((WK, 128), BF16)
    scale = 1.0 / math.sqrt(32.0)

    def by_head(o):
        return jnp.where(
            lane_head == 0,
            o[0:32],
            jnp.where(lane_head == 1, o[32:64], jnp.where(lane_head == 2, o[64:96], o[96:128])),
        )

    def window(b, masked):
        base = pl.multiple_of(b * WQ, WQ)
        first = base + jnp.clip(shift_ref[b], -HALO, WQ - HALO)
        kw = kf[pl.ds(first + HALO, WK), :].astype(BF16)
        vw = vf[pl.ds(first + HALO, WK), :].astype(BF16)
        q = qs[pl.ds(base, WQ), :]
        q4 = jnp.concatenate([q, q, q, q], axis=0) * head_mask
        s = mm(q4, kw, NT) * scale
        bias = ab[:, pl.ds(base, WQ), :].reshape(128, WK).astype(F32)
        s = s + bias
        if masked:
            j = first + p * AR + iota((1, WK), 1)
            s = jnp.where((j >= 0) & (j < AR * 16), s, -1e30)
        top = jnp.max(s, axis=-1, keepdims=True)
        w = jnp.exp(s - top).astype(BF16)
        o = mm(w, jnp.concatenate([vw, ones], axis=1))
        ms[pl.ds(base, WQ), :] = (by_head(o[:, 0:128]) / by_head(o[:, 128:256])).astype(BF16)

    def windows(lo, hi, masked):
        def group(g, carry):
            for u in range(UNROLL):
                window(g * UNROLL + u, masked)
            return carry

        lax.fori_loop(lo // UNROLL, hi // UNROLL, group, 0)

    def finish_rows(row, rows):
        r = pl.ds(row, rows)
        y = xs[pl.ds(row + HALO, rows), :].astype(F32) + mm(ms[r, :], wproj[...])
        ao[r, :] = y.astype(BF16)

    windows(24, 84, False)

    @pl.when(p > 0)
    def _():
        to_right.wait_recv()

    @pl.when(p < last)
    def _():
        to_left.wait_recv()

    @pl.when(p == 0)
    def _():
        xs[pl.ds(0, HALO), :] = jnp.zeros((HALO, 128), BF16)

    @pl.when(p == last)
    def _():
        xs[pl.ds(HALO + AR, HALO), :] = jnp.zeros((HALO, 128), BF16)

    project(0, HALO, False)
    project(HALO + AR, HALO, False)
    windows(84, 96, True)
    finish_rows(AR - TAIL, TAIL)

    @pl.when(p < last)
    def _():
        tail_right.start()

    windows(0, 24, True)

    def finish(i, carry):
        finish_rows(pl.multiple_of(i * 384, 384), 384)
        return carry

    lax.fori_loop(0, (AR - TAIL) // 384, finish, 0)
    aout_copy = pltpu.make_async_copy(ao.at[pl.ds(0, AR)], aout_h, osem.at[0])
    aout_copy.start()

    copies["agg"].wait()
    copies["ids"].wait()
    copies["tgain"].wait()
    first_token = p * TR

    def pool(row, rows):
        v = mm(ao[pl.ds(row, rows), :], wagg[...])
        hidden = (0.5 * v * (1.0 + jnp.tanh(0.5 * v))).astype(BF16)
        local = ids[:, pl.ds(row, rows)] - first_token
        hot = jnp.where(local == iota((TR, rows), 0), 1.0, 0.0)
        acc[...] += mm(hot.astype(BF16), hidden)
        osc[:, 0:128] += jnp.broadcast_to(jnp.sum(hot, axis=1, keepdims=True), (TR, 128))

    acc[...] = jnp.zeros((TR, CT), F32)
    osc[:, 0:128] = jnp.zeros((TR, 128), F32)

    def pool_own(i, carry):
        pool(pl.multiple_of(i * 768, 128), 768)
        return carry

    lax.fori_loop(0, AR // 768, pool_own, 0)

    @pl.when(p > 0)
    def _():
        ids_right.wait_recv()
        tail_right.wait_recv()

    @pl.when(p == 0)
    def _():
        ids[:, pl.ds(AR, TAIL)] = jnp.full((1, TAIL), -1, I32)
        ao[pl.ds(AR, TAIL), :] = jnp.zeros((TAIL, 128), BF16)

    pool(AR, TAIL)
    repr_f = (acc[...] / osc[:, 0:1]).astype(BF16)
    rep[...] = repr_f
    nrm[...] = normed(repr_f.astype(F32), tgain[...])

    def rows48(i):
        return pl.ds(pl.multiple_of(i * PIECE, 16), PIECE)

    def half(i):
        return pl.ds(pl.multiple_of(i * TR, 16), TR)

    outs = []
    for i in range(1, 8):
        target = lax.rem(cp + i, 8) * 2 + c
        outs.append(
            send(
                nrm.at[rows48(k)],
                kt.at[pl.ds(pl.multiple_of(c * TR + k * PIECE, 16), PIECE)],
                xsem.at[i],
                xrsem.at[k],
                target,
                cp,
            )
        )
        outs[-1].start()

    copies["wq"].wait()
    qt[...] = mm(nrm[...], wq[...]).astype(BF16)

    @pl.when(k == cp)
    def _():
        kt[half(c), :] = nrm[...]

    @pl.when(k != cp)
    def _():
        for s in range(8):
            send(
                nrm.at[rows48(0)],
                kt.at[pl.ds(pl.multiple_of(c * TR + s * PIECE, 16), PIECE)],
                xsem.at[0],
                xrsem.at[s],
                p,
                k,
            ).wait_recv()

    partner = p + 1 - 2 * c
    fwd = send(kt.at[half(c)], kt.at[half(c)], fs, fr, partner, k)
    fwd.start()
    copies["wkv"].wait()
    back = send(kt.at[half(c)], kt.at[half(1 - c)], fs, fr, partner, k)
    back.wait_recv()

    def keyvals(j, carry):
        cols = pl.ds(pl.multiple_of(j * 256, 256), 256)
        kk[:, cols] = mm(kt[...], wkv[:, cols]).astype(BF16)
        vcols = pl.ds(pl.multiple_of(j * 256 + CT, 256), 256)
        vv[:, cols] = mm(kt[...], wkv[:, vcols]).astype(BF16)
        return carry

    lax.fori_loop(0, CT // 256, keyvals, 0)
    copies["pair"].wait()
    tscale = 1.0 / math.sqrt(float(HD))
    rb = 128

    def head(h, carry):
        tile = jnp.minimum(lax.div(h * HD, 128), 4)
        lane0 = pl.multiple_of(tile * 128, 128)
        off = h * HD - lane0
        lanes = pl.ds(lane0, 256)
        keys = kk[:, lanes]
        values = vv[:, lanes]
        lane = iota((rb, 256), 1)
        mask = (lane >= off) & (lane < off + HD)
        l128 = iota((rb, 128), 1)
        for r in range(TR // rb):
            rows = pl.ds(r * rb, rb)
            q = jnp.where(mask, qt[rows, lanes].astype(F32), 0.0).astype(BF16)
            s = mm(q, keys, NT) * tscale + pbm[h, rows, :].astype(F32)
            top = jnp.max(s, axis=-1, keepdims=True)
            e = jnp.exp(s - top)
            total = jnp.sum(e, axis=-1, keepdims=True)
            o = mm(e.astype(BF16), values)
            osc[rows, lanes] = jnp.where(mask, o, osc[rows, lanes])
            mlb[rows, :] = jnp.where(
                l128 == h, top, jnp.where(l128 == h + TH, total, mlb[rows, :])
            )
        return carry

    sends = []
    for n, (lo, hi, col) in enumerate(CHUNKS):
        lax.fori_loop(lo, hi, head, 0)
        cols = pl.ds(col, 256)
        mixb[:, cols] = osc[:, cols].astype(BF16)
        for i in range(1, 8):
            peer = lax.rem(k + i, 8)
            sends.append(
                send(
                    mixb.at[rows48(peer), cols],
                    rbuf.at[i, :, cols],
                    rs.at[n, i],
                    rr.at[n, i],
                    p,
                    peer,
                )
            )
            sends[-1].start()
    for i in range(1, 8):
        peer = lax.rem(k + i, 8)
        sends.append(send(mlb.at[rows48(peer)], rml.at[i], rs.at[3, i], rr.at[3, i], p, peer))
        sends[-1].start()

    rbuf[0, :, :] = mixb[rows48(k), :]
    rml[0, :, :] = mlb[rows48(k), :]
    copies["wo"].wait()
    for copy in sends:
        copy.wait_recv()

    ml = rml[...]
    tot = pltpu.roll(ml.reshape(8 * PIECE, 128), 128 - TH, 1).reshape(8, PIECE, 128)
    real = iota((8, PIECE, 128), 2) < TH
    ml = jnp.where(real, ml, 0.0)
    tot = jnp.where(real, tot, 1.0)
    top = jnp.max(ml, axis=0, keepdims=True)
    factor = jnp.exp(ml - top)
    weight = factor / jnp.sum(factor * tot, axis=0, keepdims=True)
    weight = weight.reshape(8 * PIECE, 128)
    high = weight.astype(BF16)
    low = (weight - high.astype(F32)).astype(BF16)
    i0, j0 = iota((128, CT), 0) * HD, iota((128, CT), 1)
    expand = jnp.where((j0 >= i0) & (j0 < i0 + HD), 1.0, 0.0).astype(BF16)
    wide = (mm(high, expand) + mm(low, expand)).reshape(8, PIECE, CT)
    mix = jnp.sum(wide * rbuf[...].astype(F32), axis=0).astype(BF16)
    obuf[...] = (rep[rows48(k), :].astype(F32) + mm(mix, wo[...])).astype(BF16)
    own = pltpu.make_async_copy(obuf, tout_h.at[rows48(k)], osem.at[1])
    own.start()
    gathers = []
    for i in range(1, 8):
        peer = lax.rem(k + i, 8)
        gathers.append(send(obuf, tout_h.at[rows48(k)], gs.at[i], gr.at[i], p, peer))
        gathers[-1].start()
    own.wait()
    aout_copy.wait()
    for i in range(1, 8):
        src = lax.rem(k + 8 - i, 8)
        send(obuf, tout_h.at[rows48(src)], gs.at[i], gr.at[i], p, src).wait_recv()
    for copy in gathers + sends + outs:
        copy.wait_send()
    fwd.wait_send()

    @pl.when(p < last)
    def _():
        to_right.wait_send()
        ids_right.wait_send()
        tail_right.wait_send()

    @pl.when(p > 0)
    def _():
        to_left.wait_send()


def body(
    atoms,
    atom_gain,
    atom_qkv,
    atom_proj,
    atom_bias,
    window_shift,
    token_of_atom,
    agg_weight,
    token_gain,
    token_q,
    token_kv,
    token_o,
    pair_bias,
):
    hbm = pl.BlockSpec(memory_space=pl.ANY)
    vm = pltpu.VMEM
    dma = pltpu.SemaphoreType.DMA
    return pl.pallas_call(
        kernel,
        out_shape=(
            jax.ShapeDtypeStruct((AR, 128), BF16),
            jax.ShapeDtypeStruct((TR, CT), BF16),
        ),
        in_specs=[pl.BlockSpec(memory_space=pltpu.SMEM)] + [hbm] * 12,
        out_specs=(hbm, hbm),
        scratch_shapes=[
            vm((EXT, 128), BF16),
            vm((1, 128), F32),
            vm((128, 384), BF16),
            vm((128, 128), BF16),
            vm((4, AR, WK), BF16),
            vm((1, AR + TAIL), I32),
            vm((128, CT), BF16),
            vm((1, CT), F32),
            vm((CT, CT), BF16),
            vm((CT, 2 * CT), BF16),
            vm((CT, CT), BF16),
            vm((TH, TR, 2 * TR), BF16),
            vm((AR, 128), BF16),
            vm((EXT, 128), F32),
            vm((EXT, 128), F32),
            vm((AR, 128), BF16),
            vm((AR + TAIL, 128), BF16),
            vm((TR, CT), F32),
            vm((TR, CT), BF16),
            vm((TR, CT), BF16),
            vm((TR, CT), BF16),
            vm((2 * TR, CT), BF16),
            vm((2 * TR, CT), BF16),
            vm((2 * TR, CT), BF16),
            vm((TR, CT), F32),
            vm((TR, 128), F32),
            vm((TR, CT), BF16),
            vm((8, PIECE, CT), BF16),
            vm((8, PIECE, 128), F32),
            vm((PIECE, CT), BF16),
            dma((11,)),
            dma,
            dma((2,)),
            dma((4,)),
            dma((4,)),
            dma((8,)),
            dma((8,)),
            dma,
            dma,
            dma((4, 8)),
            dma((4, 8)),
            dma((8,)),
            dma((8,)),
        ],
        compiler_params=pltpu.CompilerParams(
            collective_id=0, has_side_effects=True, vmem_limit_bytes=60 * 1024 * 1024
        ),
    )(
        window_shift,
        atoms,
        atom_gain.reshape(1, 128),
        atom_qkv,
        atom_proj,
        atom_bias,
        token_of_atom.reshape(1, AR),
        agg_weight,
        token_gain.reshape(1, CT),
        token_q,
        token_kv,
        token_o,
        pair_bias,
    )


def solution(mesh):
    return jax.shard_map(
        body,
        mesh=mesh,
        in_specs=(
            P("pb", None),
            P(),
            P(),
            P(),
            P(None, "pb", None),
            P("pb"),
            P("pb"),
            P(),
            P(),
            P(),
            P(),
            P(),
            P(None, "pb", "ka"),
        ),
        out_specs=(P("pb", None), P("pb", None)),
        check_vma=False,
    )
```

```python
import functools
import math

import jax
import jax.numpy as jnp
from jax import lax
from jax.experimental import pallas as pl
from jax.experimental.pallas import tpu as pltpu
from jax.sharding import PartitionSpec as P

F32, BF16, I32 = jnp.float32, jnp.bfloat16, jnp.int32
AR, HALO, TAIL, WQ, WK = 3072, 64, 384, 32, 128
EXT = AR + 2 * HALO
TR, CT, TH, HD = 384, 768, 16, 48
PIECE = TR // 8
WINDOWS = AR // WQ
UNROLL = 8
CHUNKS = ((0, 6, 0), (6, 12, 256), (12, 16, 512))
FEATURES = (0, 256, 512)
NT = (((1,), (1,)), ((), ()))
NN = (((1,), (0,)), ((), ()))


def iota(shape, dim):
    return lax.broadcasted_iota(I32, shape, dim)


def mm(a, b, dims=NN):
    return lax.dot_general(a, b, dims, preferred_element_type=F32)


def normed(x, gain):
    centre = jnp.mean(x, axis=-1, keepdims=True)
    diff = x - centre
    spread = jnp.mean(diff * diff, axis=-1, keepdims=True)
    return (diff * lax.rsqrt(spread + 1e-05) * gain).astype(BF16)


def kernel(
    shift_ref,
    atoms_h,
    again_h,
    qkv_h,
    proj_h,
    abias_h,
    ids_h,
    agg_h,
    tgain_h,
    wq_h,
    wkv_h,
    wo_h,
    pair_h,
    aout_h,
    tout_h,
    xs,
    again,
    wqkv,
    wproj,
    ab,
    ids,
    wagg,
    tgain,
    wq,
    wkv,
    wo,
    pbm,
    qs,
    kf,
    vf,
    ms,
    ao,
    hot,
    hid,
    rly,
    kn,
    rep,
    nrm,
    qt,
    kt,
    kk,
    vv,
    osc,
    mlb,
    mixb,
    rbuf,
    rml,
    obuf,
    lsem,
    psem,
    osem,
    hs,
    hr,
    xsem,
    xrsem,
    rls,
    rlr,
    rfs,
    fs,
    fr,
    rs,
    rr,
    gs,
    gr,
):
    p = lax.axis_index("pb")
    k = lax.axis_index("ka")
    c = lax.rem(p, 2)
    cp = lax.div(p, 2)
    zh, zl = lax.rem(cp, 2), lax.rem(k, 2)
    outer = zh == zl
    cp_flip, k_flip, p_flip = cp + 1 - 2 * zh, k + 1 - 2 * zl, p + 2 - 4 * zh
    last = 15
    barrier = pltpu.get_barrier_semaphore()

    def dev(pb, ka):
        return {"pb": pb, "ka": ka}

    def hello(pb, ka):
        pl.semaphore_signal(barrier, inc=1, device_id=dev(pb, ka), device_id_type=pl.DeviceIdType.MESH)

    def send(src, dst, ssem, rsem, pb, ka):
        return pltpu.make_async_remote_copy(
            src_ref=src,
            dst_ref=dst,
            send_sem=ssem,
            recv_sem=rsem,
            device_id=dev(pb, ka),
            device_id_type=pl.DeviceIdType.MESH,
        )

    @pl.when(p > 0)
    def _():
        hello(p - 1, k)

    @pl.when(p < last)
    def _():
        hello(p + 1, k)

    for i in range(1, 8):
        hello(p, lax.rem(k + i, 8))

    def direct(i):
        return lax.rem(cp + i, 8) * 2 + c

    def relayed(x):
        return (2 * x + zh) * 2 + c

    @pl.when(outer)
    def _():
        for i in (2, 4, 6):
            hello(direct(i), cp)
        for x in range(4):
            hello(relayed(x), cp_flip)
        hello(p_flip, k_flip)

    @pl.when(jnp.logical_not(outer))
    def _():
        for i in range(1, 8):
            hello(direct(i), cp)
        for y in range(4):
            hello(2 * (k + 1 - 2 * zl) + c, 2 * y + 1 - zl)
            hello(2 * k + c, 2 * y + 1 - zl)

    @pl.when(jnp.logical_and(outer, k != cp))
    def _():
        for s in range(8):
            hello(2 * k + c, s)

    copies = {}

    def load(name, src, dst, sem):
        copies[name] = pltpu.make_async_copy(src, dst, sem)
        copies[name].start()

    load("atoms", atoms_h, xs.at[pl.ds(HALO, AR)], lsem.at[0])
    load("again", again_h, again, lsem.at[1])
    load("qkv", qkv_h, wqkv, lsem.at[2])
    load("abias", abias_h, ab, lsem.at[3])
    load("proj", proj_h, wproj, lsem.at[4])
    load("agg", agg_h, wagg, lsem.at[5])
    load("ids", ids_h, ids.at[:, pl.ds(0, AR)], lsem.at[6])
    load("tgain", tgain_h, tgain, lsem.at[7])
    load("wq", wq_h, wq, lsem.at[8])
    load("wkv", wkv_h, wkv, lsem.at[9])
    load("wo", wo_h, wo, lsem.at[10])
    load("pair", pair_h, pbm, psem)

    scale = 1.0 / math.sqrt(32.0)

    def project(row, rows, queries):
        x = xs[pl.ds(row, rows), :].astype(F32)
        n = normed(x, again[...])
        y = mm(n, wqkv[...])
        if queries:
            qs[pl.ds(row - HALO, rows), :] = (y[:, 0:128] * scale).astype(BF16)
        kf[pl.ds(row, rows), :] = y[:, 128:256].astype(BF16).astype(F32)
        vf[pl.ds(row, rows), :] = y[:, 256:384].astype(BF16).astype(F32)

    copies["atoms"].wait()
    copies["again"].wait()
    copies["qkv"].wait()

    def project_own(i, carry):
        project(pl.multiple_of(HALO + i * 384, 64), 384, True)
        return carry

    lax.fori_loop(0, AR // 384, project_own, 0)

    copies["abias"].wait()
    copies["proj"].wait()

    head_mask = jnp.where(
        (iota((128, 128), 0) >> 5) == (iota((128, 128), 1) >> 5), 1.0, 0.0
    ).astype(BF16)
    lane_head = iota((WQ, 128), 1) >> 5
    ones = jnp.ones((WK, 128), BF16)

    def by_head(o):
        return jnp.where(
            lane_head == 0,
            o[0:32],
            jnp.where(lane_head == 1, o[32:64], jnp.where(lane_head == 2, o[64:96], o[96:128])),
        )

    def scores(b, masked):
        base = pl.multiple_of(b * WQ, WQ)
        first = base + jnp.clip(shift_ref[b], -HALO, WQ - HALO)
        kw = kf[pl.ds(first + HALO, WK), :].astype(BF16)
        q = qs[pl.ds(base, WQ), :]
        q4 = jnp.concatenate([q, q, q, q], axis=0) * head_mask
        s = mm(q4, kw, NT) + ab[:, pl.ds(base, WQ), :].reshape(128, WK).astype(F32)
        if masked:
            j = first + p * AR + iota((1, WK), 1)
            s = jnp.where((j >= 0) & (j < AR * 16), s, -1e30)
        return base, first, s

    def windows(lo, hi, masked):
        def group(g, carry):
            part = [scores(g * UNROLL + u, masked) for u in range(UNROLL)]
            tops = [jnp.max(s, axis=-1, keepdims=True) for _, _, s in part]
            weights = [jnp.exp(s - t).astype(BF16) for (_, _, s), t in zip(part, tops)]
            mixes = []
            for (_, first, _), w in zip(part, weights):
                vw = vf[pl.ds(first + HALO, WK), :].astype(BF16)
                mixes.append(mm(w, jnp.concatenate([vw, ones], axis=1)))
            for (base, _, _), o in zip(part, mixes):
                ms[pl.ds(base, WQ), :] = (
                    by_head(o[:, 0:128]) / by_head(o[:, 128:256])
                ).astype(BF16)
            return carry

        lax.fori_loop(lo // UNROLL, hi // UNROLL, group, 0)

    def finish_rows(row, rows):
        r = pl.ds(row, rows)
        y = xs[pl.ds(row + HALO, rows), :].astype(F32) + mm(ms[r, :], wproj[...])
        ao[r, :] = y.astype(BF16)

    windows(24, 56, False)

    greeted = (
        14
        + jnp.where(p > 0, 1, 0)
        + jnp.where(p < last, 1, 0)
        + jnp.where(k != cp, 8, 0)
        + jnp.where(outer, 1, 0)
    )
    pl.semaphore_wait(barrier, greeted)
    right = jnp.minimum(p + 1, last)
    left = jnp.maximum(p - 1, 0)
    to_right = send(
        atoms_h.at[pl.ds(AR - HALO, HALO)], xs.at[pl.ds(0, HALO)], hs.at[0], hr.at[0], right, k
    )
    to_left = send(
        atoms_h.at[pl.ds(0, HALO)], xs.at[pl.ds(HALO + AR, HALO)], hs.at[1], hr.at[1], left, k
    )
    ids_right = send(
        ids_h.at[:, pl.ds(AR - TAIL, TAIL)], ids.at[:, pl.ds(AR, TAIL)], hs.at[2], hr.at[2], right, k
    )
    tail_right = send(
        ao.at[pl.ds(AR - TAIL, TAIL)], ao.at[pl.ds(AR, TAIL)], hs.at[3], hr.at[3], right, k
    )

    @pl.when(p < last)
    def _():
        to_right.start()
        ids_right.start()

    @pl.when(p > 0)
    def _():
        to_left.start()

    windows(56, 80, False)

    @pl.when(p > 0)
    def _():
        to_right.wait_recv()

    @pl.when(p < last)
    def _():
        to_left.wait_recv()

    @pl.when(p == 0)
    def _():
        xs[pl.ds(0, HALO), :] = jnp.zeros((HALO, 128), BF16)

    @pl.when(p == last)
    def _():
        xs[pl.ds(HALO + AR, HALO), :] = jnp.zeros((HALO, 128), BF16)

    project(0, HALO, False)
    project(HALO + AR, HALO, False)
    windows(80, 96, True)
    finish_rows(AR - TAIL, TAIL)

    @pl.when(p < last)
    def _():
        tail_right.start()

    windows(0, 24, True)

    def finish(i, carry):
        finish_rows(pl.multiple_of(i * 384, 384), 384)
        return carry

    lax.fori_loop(0, (AR - TAIL) // 384, finish, 0)
    aout_copy = pltpu.make_async_copy(ao.at[pl.ds(0, AR)], aout_h, osem.at[0])
    aout_copy.start()

    copies["agg"].wait()
    copies["ids"].wait()
    copies["tgain"].wait()
    first_token = p * TR

    def slots(row, rows):
        local = ids[:, pl.ds(row, rows)] - first_token
        hits = jnp.where(local == iota((TR, rows), 0), 1.0, 0.0)
        hot[:, pl.ds(row, rows)] = hits.astype(BF16)
        mlb[...] += hits[:, 0:128] + hits[:, 128:256] + hits[:, 256:384]

    def slots_own(i, carry):
        slots(pl.multiple_of(i * 384, 128), 384)
        return carry

    mlb[...] = jnp.zeros((TR, 128), F32)
    lax.fori_loop(0, AR // 384, slots_own, 0)

    @pl.when(p > 0)
    def _():
        ids_right.wait_recv()
        tail_right.wait_recv()

    @pl.when(p == 0)
    def _():
        ids[:, pl.ds(AR, TAIL)] = jnp.full((1, TAIL), -1, I32)
        ao[pl.ds(AR, TAIL), :] = jnp.zeros((TAIL, 128), BF16)

    slots(AR, TAIL)
    counts = jnp.sum(mlb[...], axis=1, keepdims=True)

    def rows48(i):
        return pl.ds(pl.multiple_of(i * PIECE, 16), PIECE)

    def landing(core, source):
        return pl.ds(pl.multiple_of(core * TR + source * PIECE, 16), PIECE)

    def half(i):
        return pl.ds(pl.multiple_of(i * TR, 16), TR)

    directs, hops, onward = [], [], []
    for f, col in enumerate(FEATURES):
        cols = pl.ds(col, 256)
        directs.append(
            [
                send(
                    rep.at[rows48(k), cols],
                    kt.at[landing(c, k), cols],
                    xsem.at[f, i],
                    xrsem.at[f, k],
                    direct(i),
                    cp,
                )
                for i in range(1, 8)
            ]
        )
        hops.append(
            send(rep.at[rows48(k), cols], rly.at[:, cols], rls.at[f], rlr.at[f], p_flip, k_flip)
        )
        onward.append(
            [
                send(
                    rly.at[:, cols],
                    kt.at[landing(c, k_flip), cols],
                    rfs.at[f, x],
                    xrsem.at[f, k_flip],
                    relayed(x),
                    cp_flip,
                )
                for x in range(4)
            ]
        )

    def pass_on(f):
        @pl.when(outer)
        def _():
            hops[f].wait_recv()
            for copy in onward[f]:
                copy.start()

    for f, col in enumerate(FEATURES):
        cols = pl.ds(col, 256)

        def hidden(i, carry):
            r = pl.ds(pl.multiple_of(i * 384, 128), 384)
            v = mm(ao[r, :], wagg[:, cols])
            hid[r, :] = (0.5 * v * (1.0 + jnp.tanh(0.5 * v))).astype(BF16)
            return carry

        lax.fori_loop(0, (AR + TAIL) // 384, hidden, 0)
        rep[:, cols] = (mm(hot[...], hid[...]) / counts).astype(BF16)

        @pl.when(outer)
        def _():
            for i in (2, 4, 6):
                directs[f][i - 1].start()
            hops[f].start()

        @pl.when(jnp.logical_not(outer))
        def _():
            for copy in directs[f]:
                copy.start()

        if f > 0:
            pass_on(f - 1)

    tscale = 1.0 / math.sqrt(float(HD))
    copies["wq"].wait()
    nrm[...] = normed(rep[...].astype(F32), tgain[...].reshape(1, CT))
    pass_on(len(FEATURES) - 1)
    qt[...] = (mm(nrm[...], wq[...]) * tscale).astype(BF16)
    partner = p + 1 - 2 * c

    @pl.when(k == cp)
    def _():
        kt[half(c), :] = rep[...]

    fwds, backs = [], []
    for f, col in enumerate(FEATURES):
        cols = pl.ds(col, 256)
        fwds.append(
            send(kt.at[half(c), cols], kt.at[half(c), cols], fs.at[f], fr.at[f], partner, k)
        )
        backs.append(
            send(kt.at[half(c), cols], kt.at[half(1 - c), cols], fs.at[f], fr.at[f], partner, k)
        )

        @pl.when(k != cp)
        def _():
            for s in range(8):
                send(
                    rep.at[rows48(0), cols],
                    kt.at[landing(c, s), cols],
                    xsem.at[f, 0],
                    xrsem.at[f, s],
                    partner,
                    k,
                ).wait_recv()

        fwds[f].start()

    copies["wkv"].wait()
    for copy in backs:
        copy.wait_recv()

    def key_norm(i, carry):
        r = pl.ds(pl.multiple_of(i * 128, 128), 128)
        kn[r, :] = normed(kt[r, :].astype(F32), tgain[...].reshape(1, CT))
        return carry

    lax.fori_loop(0, 2 * TR // 128, key_norm, 0)

    def keyvals(j, carry):
        cols = pl.ds(pl.multiple_of(j * 256, 256), 256)
        kk[:, cols] = mm(kn[...], wkv[:, cols]).astype(BF16)
        vcols = pl.ds(pl.multiple_of(j * 256 + CT, 256), 256)
        vv[:, cols] = mm(kn[...], wkv[:, vcols]).astype(BF16)
        return carry

    lax.fori_loop(0, CT // 256, keyvals, 0)
    copies["pair"].wait()
    rb = 128
    l128 = iota((rb, 128), 1)

    def heads(pair, carry):
        work = []
        for u in range(2):
            h = pair * 2 + u
            lane0 = pl.multiple_of(jnp.minimum(lax.div(h * HD, 128), 4) * 128, 128)
            off = h * HD - lane0
            lanes = pl.ds(lane0, 256)
            lane = iota((1, 256), 1)
            mask = (lane >= off) & (lane < off + HD)
            values = jnp.where(mask, vv[:, lanes].astype(F32), 1.0).astype(BF16)
            for r in range(TR // rb):
                work.append((h, lanes, mask, values, pl.ds(r * rb, rb)))

        def score(h, lanes, mask, values, r):
            q = jnp.where(mask, qt[r, lanes].astype(F32), 0.0).astype(BF16)
            return mm(q, kk[:, lanes], NT) + pbm[h, r, :].astype(F32)

        def store(h, lanes, mask, r, top, o):
            osc[r, lanes] = jnp.where(mask, o, osc[r, lanes])
            total = jnp.where(mask[:, 0:128], o[:, 128:256], o[:, 0:128])
            mlb[r, :] = jnp.where(l128 == h, top, jnp.where(l128 == h + TH, total, mlb[r, :]))

        ahead = score(*work[0])
        done = None
        for n, (h, lanes, mask, values, r) in enumerate(work):
            s = ahead
            if n + 1 < len(work):
                ahead = score(*work[n + 1])
            top = jnp.max(s, axis=-1, keepdims=True)
            o = mm(jnp.exp(s - top).astype(BF16), values)
            if done is not None:
                store(*done)
            done = (h, lanes, mask, r, top, o)
        store(*done)
        return carry

    sends = []
    for n, (lo, hi, col) in enumerate(CHUNKS):
        lax.fori_loop(lo // 2, hi // 2, heads, 0)
        cols = pl.ds(col, 256)
        mixb[:, cols] = osc[:, cols].astype(BF16)
        for i in range(1, 8):
            peer = lax.rem(k + i, 8)
            sends.append(
                send(
                    mixb.at[rows48(peer), cols],
                    rbuf.at[i, :, cols],
                    rs.at[n, i],
                    rr.at[n, i],
                    p,
                    peer,
                )
            )
            sends[-1].start()
    for i in range(1, 8):
        peer = lax.rem(k + i, 8)
        sends.append(send(mlb.at[rows48(peer)], rml.at[i], rs.at[3, i], rr.at[3, i], p, peer))
        sends[-1].start()

    rbuf[0, :, :] = mixb[rows48(k), :]
    rml[0, :, :] = mlb[rows48(k), :]
    copies["wo"].wait()
    for copy in sends:
        copy.wait_recv()

    ml = rml[...]
    tot = pltpu.roll(ml.reshape(8 * PIECE, 128), 128 - TH, 1).reshape(8, PIECE, 128)
    real = iota((8, PIECE, 128), 2) < TH
    ml = jnp.where(real, ml, 0.0)
    tot = jnp.where(real, tot, 1.0)
    top = jnp.max(ml, axis=0, keepdims=True)
    factor = jnp.exp(ml - top)
    weight = factor / jnp.sum(factor * tot, axis=0, keepdims=True)
    weight = weight.reshape(8 * PIECE, 128)
    high = weight.astype(BF16)
    low = (weight - high.astype(F32)).astype(BF16)
    i0, j0 = iota((128, CT), 0) * HD, iota((128, CT), 1)
    expand = jnp.where((j0 >= i0) & (j0 < i0 + HD), 1.0, 0.0).astype(BF16)
    wide = (mm(high, expand) + mm(low, expand)).reshape(8, PIECE, CT)
    mix = jnp.sum(wide * rbuf[...].astype(F32), axis=0).astype(BF16)
    obuf[...] = (rep[rows48(k), :].astype(F32) + mm(mix, wo[...])).astype(BF16)
    own = pltpu.make_async_copy(obuf, tout_h.at[rows48(k)], osem.at[1])
    own.start()
    gathers = []
    for i in range(1, 8):
        peer = lax.rem(k + i, 8)
        gathers.append(send(obuf, tout_h.at[rows48(k)], gs.at[i], gr.at[i], p, peer))
        gathers[-1].start()
    own.wait()
    aout_copy.wait()
    for i in range(1, 8):
        src = lax.rem(k + 8 - i, 8)
        send(obuf, tout_h.at[rows48(src)], gs.at[i], gr.at[i], p, src).wait_recv()
    for copy in gathers + sends + fwds:
        copy.wait_send()

    @pl.when(outer)
    def _():
        for f in range(len(FEATURES)):
            for i in (2, 4, 6):
                directs[f][i - 1].wait_send()
            hops[f].wait_send()
            for copy in onward[f]:
                copy.wait_send()

    @pl.when(jnp.logical_not(outer))
    def _():
        for f in range(len(FEATURES)):
            for copy in directs[f]:
                copy.wait_send()

    @pl.when(p < last)
    def _():
        to_right.wait_send()
        ids_right.wait_send()
        tail_right.wait_send()

    @pl.when(p > 0)
    def _():
        to_left.wait_send()


def body(
    atoms,
    atom_gain,
    atom_qkv,
    atom_proj,
    atom_bias,
    window_shift,
    token_of_atom,
    agg_weight,
    token_gain,
    token_q,
    token_kv,
    token_o,
    pair_bias,
):
    hbm = pl.BlockSpec(memory_space=pl.ANY)
    vm = pltpu.VMEM
    dma = pltpu.SemaphoreType.DMA
    return pl.pallas_call(
        kernel,
        out_shape=(
            jax.ShapeDtypeStruct((AR, 128), BF16),
            jax.ShapeDtypeStruct((TR, CT), BF16),
        ),
        in_specs=[pl.BlockSpec(memory_space=pltpu.SMEM)] + [hbm] * 12,
        out_specs=(hbm, hbm),
        scratch_shapes=[
            vm((EXT, 128), BF16),
            vm((1, 128), F32),
            vm((128, 384), BF16),
            vm((128, 128), BF16),
            vm((4, AR, WK), BF16),
            vm((1, AR + TAIL), I32),
            vm((128, CT), BF16),
            vm((CT,), F32),
            vm((CT, CT), BF16),
            vm((CT, 2 * CT), BF16),
            vm((CT, CT), BF16),
            vm((TH, TR, 2 * TR), BF16),
            vm((AR, 128), BF16),
            vm((EXT, 128), F32),
            vm((EXT, 128), F32),
            vm((AR, 128), BF16),
            vm((AR + TAIL, 128), BF16),
            vm((TR, AR + TAIL), BF16),
            vm((AR + TAIL, 256), BF16),
            vm((PIECE, CT), BF16),
            vm((2 * TR, CT), BF16),
            vm((TR, CT), BF16),
            vm((TR, CT), BF16),
            vm((TR, CT), BF16),
            vm((2 * TR, CT), BF16),
            vm((2 * TR, CT), BF16),
            vm((2 * TR, CT), BF16),
            vm((TR, CT), F32),
            vm((TR, 128), F32),
            vm((TR, CT), BF16),
            vm((8, PIECE, CT), BF16),
            vm((8, PIECE, 128), F32),
            vm((PIECE, CT), BF16),
            dma((11,)),
            dma,
            dma((2,)),
            dma((4,)),
            dma((4,)),
            dma((3, 8)),
            dma((3, 8)),
            dma((3,)),
            dma((3,)),
            dma((3, 4)),
            dma((3,)),
            dma((3,)),
            dma((4, 8)),
            dma((4, 8)),
            dma((8,)),
            dma((8,)),
        ],
        compiler_params=pltpu.CompilerParams(
            collective_id=0, has_side_effects=True, vmem_limit_bytes=60 * 1024 * 1024
        ),
    )(
        window_shift,
        atoms,
        atom_gain.reshape(1, 128),
        atom_qkv,
        atom_proj,
        atom_bias,
        token_of_atom.reshape(1, AR),
        agg_weight,
        token_gain,
        token_q,
        token_kv,
        token_o,
        pair_bias,
    )


def solution(mesh):
    return jax.shard_map(
        body,
        mesh=mesh,
        in_specs=(
            P("pb", None),
            P(),
            P(),
            P(),
            P(None, "pb", None),
            P("pb"),
            P("pb"),
            P(),
            P(),
            P(),
            P(),
            P(),
            P(None, "pb", "ka"),
        ),
        out_specs=(P("pb", None), P("pb", None)),
        check_vma=False,
    )
```

```python
import functools
import math

import jax
import jax.numpy as jnp
from jax import lax
from jax.experimental import pallas as pl
from jax.experimental.pallas import tpu as pltpu
from jax.sharding import PartitionSpec as P

F32, BF16, I32 = jnp.float32, jnp.bfloat16, jnp.int32
AR, HALO, TAIL, WQ, WK = 3072, 64, 384, 32, 128
EXT = AR + 2 * HALO
TR, CT, TH, HD = 384, 768, 16, 48
PIECE = TR // 8
PARTS = ((0, 256), (256, 128))
WINDOWS = AR // WQ
UNROLL = 8
CHUNKS = (((0, 8, 0, 384), (8, 14, 384, 256), (14, 16, 640, 128)), ((0, 8, 0, 384), (8, 16, 384, 384)))
FEATURES = (0, 256, 512)
NT = (((1,), (1,)), ((), ()))
NN = (((1,), (0,)), ((), ()))


def iota(shape, dim):
    return lax.broadcasted_iota(I32, shape, dim)


def mm(a, b, dims=NN):
    return lax.dot_general(a, b, dims, preferred_element_type=F32)


def normed(x, gain):
    centre = jnp.mean(x, axis=-1, keepdims=True)
    diff = x - centre
    spread = jnp.mean(diff * diff, axis=-1, keepdims=True)
    return (diff * lax.rsqrt(spread + 1e-05) * gain).astype(BF16)


def kernel(
    shift_ref,
    atoms_h,
    again_h,
    qkv_h,
    proj_h,
    abias_h,
    ids_h,
    agg_h,
    tgain_h,
    wq_h,
    wkv_h,
    wo_h,
    pair_h,
    aout_h,
    tout_h,
    xs,
    again,
    wqkv,
    wproj,
    ab,
    ids,
    wagg,
    tgain,
    wq,
    wkv,
    wo,
    pbm,
    qs,
    kf,
    vf,
    ms,
    ao,
    hot,
    hid,
    rly,
    kn,
    rep,
    nrm,
    qt,
    kt,
    kk,
    vv,
    osc,
    mlb,
    mixb,
    rbuf_a,
    rbuf_b,
    mlp_a,
    mlp_b,
    rml_a,
    rml_b,
    obuf_a,
    obuf_b,
    lsem,
    psem,
    osem,
    hs,
    hr,
    xsem,
    xrsem,
    rls,
    rlr,
    rfs,
    fs,
    fr,
    rs,
    rr,
    gs,
    gr,
):
    rbuf, mlp, rml, obuf = (rbuf_a, rbuf_b), (mlp_a, mlp_b), (rml_a, rml_b), (obuf_a, obuf_b)
    p = lax.axis_index("pb")
    k = lax.axis_index("ka")
    c = lax.rem(p, 2)
    cp = lax.div(p, 2)
    zh, zl = lax.rem(cp, 2), lax.rem(k, 2)
    outer = zh == zl
    cp_flip, k_flip, p_flip = cp + 1 - 2 * zh, k + 1 - 2 * zl, p + 2 - 4 * zh
    last = 15
    barrier = pltpu.get_barrier_semaphore()

    def dev(pb, ka):
        return {"pb": pb, "ka": ka}

    def hello(pb, ka):
        pl.semaphore_signal(barrier, inc=1, device_id=dev(pb, ka), device_id_type=pl.DeviceIdType.MESH)

    def send(src, dst, ssem, rsem, pb, ka):
        return pltpu.make_async_remote_copy(
            src_ref=src,
            dst_ref=dst,
            send_sem=ssem,
            recv_sem=rsem,
            device_id=dev(pb, ka),
            device_id_type=pl.DeviceIdType.MESH,
        )

    @pl.when(p > 0)
    def _():
        hello(p - 1, k)

    @pl.when(p < last)
    def _():
        hello(p + 1, k)

    for i in range(1, 8):
        hello(p, lax.rem(k + i, 8))

    def direct(i):
        return lax.rem(cp + i, 8) * 2 + c

    def relayed(x):
        return (2 * x + zh) * 2 + c

    @pl.when(outer)
    def _():
        for i in (2, 4, 6):
            hello(direct(i), cp)
        for x in range(4):
            hello(relayed(x), cp_flip)
        hello(p_flip, k_flip)

    @pl.when(jnp.logical_not(outer))
    def _():
        for i in range(1, 8):
            hello(direct(i), cp)
        for y in range(4):
            hello(2 * (k + 1 - 2 * zl) + c, 2 * y + 1 - zl)
            hello(2 * k + c, 2 * y + 1 - zl)

    @pl.when(jnp.logical_and(outer, k != cp))
    def _():
        for s in range(8):
            hello(2 * k + c, s)

    copies = {}

    def load(name, src, dst, sem):
        copies[name] = pltpu.make_async_copy(src, dst, sem)
        copies[name].start()

    load("atoms", atoms_h, xs.at[pl.ds(HALO, AR)], lsem.at[0])
    load("again", again_h, again, lsem.at[1])
    load("qkv", qkv_h, wqkv, lsem.at[2])
    load("abias", abias_h, ab, lsem.at[3])
    load("proj", proj_h, wproj, lsem.at[4])
    load("agg", agg_h, wagg, lsem.at[5])
    load("ids", ids_h, ids.at[:, pl.ds(0, AR)], lsem.at[6])
    load("tgain", tgain_h, tgain, lsem.at[7])
    load("wq", wq_h, wq, lsem.at[8])
    load("wkv", wkv_h, wkv, lsem.at[9])
    load("wo", wo_h, wo, lsem.at[10])
    load("pair", pair_h, pbm, psem)

    scale = 1.0 / math.sqrt(32.0)

    def project(row, rows, queries):
        x = xs[pl.ds(row, rows), :].astype(F32)
        n = normed(x, again[...])
        y = mm(n, wqkv[...])
        if queries:
            qs[pl.ds(row - HALO, rows), :] = (y[:, 0:128] * scale).astype(BF16)
        kf[pl.ds(row, rows), :] = y[:, 128:256].astype(BF16).astype(F32)
        vf[pl.ds(row, rows), :] = y[:, 256:384].astype(BF16).astype(F32)

    copies["atoms"].wait()
    copies["again"].wait()
    copies["qkv"].wait()

    def project_own(i, carry):
        project(pl.multiple_of(HALO + i * 384, 64), 384, True)
        return carry

    lax.fori_loop(0, AR // 384, project_own, 0)

    copies["abias"].wait()
    copies["proj"].wait()

    head_mask = jnp.where(
        (iota((128, 128), 0) >> 5) == (iota((128, 128), 1) >> 5), 1.0, 0.0
    ).astype(BF16)
    lane_head = iota((WQ, 128), 1) >> 5
    ones = jnp.ones((WK, 128), BF16)

    def by_head(o):
        return jnp.where(
            lane_head == 0,
            o[0:32],
            jnp.where(lane_head == 1, o[32:64], jnp.where(lane_head == 2, o[64:96], o[96:128])),
        )

    def scores(b, masked):
        base = pl.multiple_of(b * WQ, WQ)
        first = base + jnp.clip(shift_ref[b], -HALO, WQ - HALO)
        kw = kf[pl.ds(first + HALO, WK), :].astype(BF16)
        q = qs[pl.ds(base, WQ), :]
        q4 = jnp.concatenate([q, q, q, q], axis=0) * head_mask
        s = mm(q4, kw, NT) + ab[:, pl.ds(base, WQ), :].reshape(128, WK).astype(F32)
        if masked:
            j = first + p * AR + iota((1, WK), 1)
            s = jnp.where((j >= 0) & (j < AR * 16), s, -1e30)
        return base, first, s

    def windows(lo, hi, masked):
        def group(g, carry):
            part = [scores(g * UNROLL + u, masked) for u in range(UNROLL)]
            tops = [jnp.max(s, axis=-1, keepdims=True) for _, _, s in part]
            weights = [jnp.exp(s - t).astype(BF16) for (_, _, s), t in zip(part, tops)]
            mixes = []
            for (_, first, _), w in zip(part, weights):
                vw = vf[pl.ds(first + HALO, WK), :].astype(BF16)
                mixes.append(mm(w, jnp.concatenate([vw, ones], axis=1)))
            for (base, _, _), o in zip(part, mixes):
                ms[pl.ds(base, WQ), :] = (
                    by_head(o[:, 0:128]) / by_head(o[:, 128:256])
                ).astype(BF16)
            return carry

        lax.fori_loop(lo // UNROLL, hi // UNROLL, group, 0)

    def finish_rows(row, rows):
        r = pl.ds(row, rows)
        y = xs[pl.ds(row + HALO, rows), :].astype(F32) + mm(ms[r, :], wproj[...])
        ao[r, :] = y.astype(BF16)

    windows(8, 64, False)

    greeted = (
        14
        + jnp.where(p > 0, 1, 0)
        + jnp.where(p < last, 1, 0)
        + jnp.where(k != cp, 8, 0)
        + jnp.where(outer, 1, 0)
    )
    pl.semaphore_wait(barrier, greeted)
    right = jnp.minimum(p + 1, last)
    left = jnp.maximum(p - 1, 0)
    to_right = send(
        atoms_h.at[pl.ds(AR - HALO, HALO)], xs.at[pl.ds(0, HALO)], hs.at[0], hr.at[0], right, k
    )
    to_left = send(
        atoms_h.at[pl.ds(0, HALO)], xs.at[pl.ds(HALO + AR, HALO)], hs.at[1], hr.at[1], left, k
    )
    ids_right = send(
        ids_h.at[:, pl.ds(AR - TAIL, TAIL)], ids.at[:, pl.ds(AR, TAIL)], hs.at[2], hr.at[2], right, k
    )
    tail_right = send(
        ao.at[pl.ds(AR - TAIL, TAIL)], ao.at[pl.ds(AR, TAIL)], hs.at[3], hr.at[3], right, k
    )

    @pl.when(p < last)
    def _():
        to_right.start()
        ids_right.start()

    @pl.when(p > 0)
    def _():
        to_left.start()

    windows(64, 80, False)

    @pl.when(p > 0)
    def _():
        to_right.wait_recv()

    @pl.when(p < last)
    def _():
        to_left.wait_recv()

    @pl.when(p == 0)
    def _():
        xs[pl.ds(0, HALO), :] = jnp.zeros((HALO, 128), BF16)

    @pl.when(p == last)
    def _():
        xs[pl.ds(HALO + AR, HALO), :] = jnp.zeros((HALO, 128), BF16)

    project(0, HALO, False)
    project(HALO + AR, HALO, False)
    windows(80, 96, True)
    finish_rows(AR - TAIL, TAIL)

    @pl.when(p < last)
    def _():
        tail_right.start()

    windows(0, 8, True)

    def finish(i, carry):
        finish_rows(pl.multiple_of(i * 384, 384), 384)
        return carry

    lax.fori_loop(0, (AR - TAIL) // 384, finish, 0)
    aout_copy = pltpu.make_async_copy(ao.at[pl.ds(0, AR)], aout_h, osem.at[0])
    aout_copy.start()

    copies["agg"].wait()
    copies["ids"].wait()
    copies["tgain"].wait()
    first_token = p * TR

    def slots(row, rows):
        local = ids[:, pl.ds(row, rows)] - first_token
        hits = jnp.where(local == iota((TR, rows), 0), 1.0, 0.0)
        hot[:, pl.ds(row, rows)] = hits.astype(BF16)
        mlb[...] += hits[:, 0:128] + hits[:, 128:256] + hits[:, 256:384]

    def slots_own(i, carry):
        slots(pl.multiple_of(i * 384, 128), 384)
        return carry

    mlb[...] = jnp.zeros((TR, 128), F32)
    lax.fori_loop(0, AR // 384, slots_own, 0)

    def tail_rows():
        @pl.when(p > 0)
        def _():
            ids_right.wait_recv()
            tail_right.wait_recv()

        @pl.when(p == 0)
        def _():
            ids[:, pl.ds(AR, TAIL)] = jnp.full((1, TAIL), -1, I32)
            ao[pl.ds(AR, TAIL), :] = jnp.zeros((TAIL, 128), BF16)

        slots(AR, TAIL)

    def rows48(i):
        return pl.ds(pl.multiple_of(i * PIECE, 16), PIECE)

    def landing(core, source):
        return pl.ds(pl.multiple_of(core * TR + source * PIECE, 16), PIECE)

    def half(i):
        return pl.ds(pl.multiple_of(i * TR, 16), TR)

    directs, hops, onward = [], [], []
    for f, col in enumerate(FEATURES):
        cols = pl.ds(col, 256)
        directs.append(
            [
                send(
                    rep.at[rows48(k), cols],
                    kt.at[landing(c, k), cols],
                    xsem.at[f, i],
                    xrsem.at[f, k],
                    direct(i),
                    cp,
                )
                for i in range(1, 8)
            ]
        )
        hops.append(
            send(rep.at[rows48(k), cols], rly.at[:, cols], rls.at[f], rlr.at[f], p_flip, k_flip)
        )
        onward.append(
            [
                send(
                    rly.at[:, cols],
                    kt.at[landing(c, k_flip), cols],
                    rfs.at[f, x],
                    xrsem.at[f, k_flip],
                    relayed(x),
                    cp_flip,
                )
                for x in range(4)
            ]
        )

    def pass_on(f):
        @pl.when(outer)
        def _():
            hops[f].wait_recv()
            for copy in onward[f]:
                copy.start()

    for f, col in enumerate(FEATURES):
        cols = pl.ds(col, 256)

        def hidden(i, carry):
            r = pl.ds(i * 384 if isinstance(i, int) else pl.multiple_of(i * 384, 128), 384)
            v = mm(ao[r, :], wagg[:, cols])
            hid[r, :] = (0.5 * v * (1.0 + jnp.tanh(0.5 * v))).astype(BF16)
            return carry

        if f == 0:
            lax.fori_loop(0, AR // 384, hidden, 0)
            tail_rows()
            hidden(AR // 384, 0)
            counts = jnp.sum(mlb[...], axis=1, keepdims=True)
        else:
            lax.fori_loop(0, (AR + TAIL) // 384, hidden, 0)
        rep[:, cols] = (mm(hot[...], hid[...]) / counts).astype(BF16)

        @pl.when(outer)
        def _():
            for i in (2, 4, 6):
                directs[f][i - 1].start()
            hops[f].start()

        @pl.when(jnp.logical_not(outer))
        def _():
            for copy in directs[f]:
                copy.start()

        if f > 0:
            pass_on(f - 1)

    tscale = 1.0 / math.sqrt(float(HD))
    copies["wq"].wait()
    nrm[...] = normed(rep[...].astype(F32), tgain[...].reshape(1, CT))
    pass_on(len(FEATURES) - 1)
    qt[...] = (mm(nrm[...], wq[...]) * tscale).astype(BF16)
    partner = p + 1 - 2 * c

    @pl.when(k == cp)
    def _():
        kt[half(c), :] = rep[...]

    fwds, backs = [], []
    for f, col in enumerate(FEATURES):
        cols = pl.ds(col, 256)
        fwds.append(
            send(kt.at[half(c), cols], kt.at[half(c), cols], fs.at[f], fr.at[f], partner, k)
        )
        backs.append(
            send(kt.at[half(c), cols], kt.at[half(1 - c), cols], fs.at[f], fr.at[f], partner, k)
        )

        @pl.when(k != cp)
        def _():
            for s in range(8):
                send(
                    rep.at[rows48(0), cols],
                    kt.at[landing(c, s), cols],
                    xsem.at[f, 0],
                    xrsem.at[f, s],
                    partner,
                    k,
                ).wait_recv()

        fwds[f].start()

    copies["wkv"].wait()
    for copy in backs:
        copy.wait_recv()

    def key_norm(i, carry):
        r = pl.ds(pl.multiple_of(i * 128, 128), 128)
        kn[r, :] = normed(kt[r, :].astype(F32), tgain[...].reshape(1, CT))
        return carry

    lax.fori_loop(0, 2 * TR // 128, key_norm, 0)

    def keyvals(j, carry):
        cols = pl.ds(pl.multiple_of(j * 256, 256), 256)
        kk[:, cols] = mm(kn[...], wkv[:, cols]).astype(BF16)
        vcols = pl.ds(pl.multiple_of(j * 256 + CT, 256), 256)
        vv[:, cols] = mm(kn[...], wkv[:, vcols]).astype(BF16)
        return carry

    lax.fori_loop(0, CT // 256, keyvals, 0)
    copies["pair"].wait()
    rb = 128
    l128 = iota((rb, 128), 1)
    copies["wo"].wait()

    def make_heads(row, rows, together):
        def heads(group, carry):
            work = []
            for u in range(together):
                h = group * together + u
                lane0 = pl.multiple_of(jnp.minimum(lax.div(h * HD, 128), 4) * 128, 128)
                off = h * HD - lane0
                lanes = pl.ds(lane0, 256)
                lane = iota((1, 256), 1)
                mask = (lane >= off) & (lane < off + HD)
                values = jnp.where(mask, vv[:, lanes].astype(F32), 1.0).astype(BF16)
                for r in range(row, row + rows, rb):
                    work.append((h, lanes, mask, values, pl.ds(r, rb)))

            def score(h, lanes, mask, values, r):
                q = jnp.where(mask, qt[r, lanes].astype(F32), 0.0).astype(BF16)
                return mm(q, kk[:, lanes], NT) + pbm[h, r, :].astype(F32)

            def store(h, lanes, mask, r, top, o):
                osc[r, lanes] = jnp.where(mask, o, osc[r, lanes])
                total = jnp.where(mask[:, 0:128], o[:, 128:256], o[:, 0:128])
                mlb[r, :] = jnp.where(l128 == h, top, jnp.where(l128 == h + TH, total, mlb[r, :]))

            ahead = score(*work[0])
            done = None
            for n, (h, lanes, mask, values, r) in enumerate(work):
                s = ahead
                if n + 1 < len(work):
                    ahead = score(*work[n + 1])
                top = jnp.max(s, axis=-1, keepdims=True)
                o = mm(jnp.exp(s - top).astype(BF16), values)
                if done is not None:
                    store(*done)
                done = (h, lanes, mask, r, top, o)
            store(*done)
            return carry

        return heads

    i0, j0 = iota((128, CT), 0) * HD, iota((128, CT), 1)
    expand = jnp.where((j0 >= i0) & (j0 < i0 + HD), 1.0, 0.0).astype(BF16)
    sends, gathers = ([], []), ([], [])

    def owned(part, owner):
        row, rows = PARTS[part]
        return pl.ds(pl.multiple_of(row + owner * (rows // 8), 16), rows // 8)

    def attend(part, n):
        row, rows = PARTS[part]
        lo, hi, col, width = CHUNKS[part][n]
        together = 512 // rows
        lax.fori_loop(lo // together, hi // together, make_heads(row, rows, together), 0)
        cols = pl.ds(col, width)
        mixb[pl.ds(row, rows), cols] = osc[pl.ds(row, rows), cols].astype(BF16)
        for i in range(1, 8):
            peer = lax.rem(k + i, 8)
            copy = send(
                mixb.at[owned(part, peer), cols],
                rbuf[part].at[i, :, cols],
                rs.at[part, n, i],
                rr.at[part, n, i],
                p,
                peer,
            )
            copy.start()
            sends[part].append(copy)

    def share_sums(part):
        row, rows = PARTS[part]
        count = rows // 64
        grouped = mlb[pl.ds(row, rows), :].reshape(8, count, 8, 128)
        lane = iota((8, 8, 128), 2)
        packed = grouped[:, 0]
        for j in range(1, count):
            turned = pltpu.roll(grouped[:, j].reshape(64, 128), 32 * j, 1).reshape(8, 8, 128)
            packed = jnp.where(lane >= 32 * j, turned, packed)
        mlp[part][...] = packed
        for i in range(1, 8):
            peer = lax.rem(k + i, 8)
            copy = send(
                mlp[part].at[peer], rml[part].at[i], rs.at[part, 3, i], rr.at[part, 3, i], p, peer
            )
            copy.start()
            sends[part].append(copy)

    def merge(part):
        row, rows = PARTS[part]
        piece, count = rows // 8, rows // 64
        rbuf[part][0, :, :] = mixb[owned(part, k), :]
        rml[part][0, :, :] = mlp[part][k, :, :]
        for copy in sends[part]:
            copy.wait_recv()
        packed = rml[part][...].reshape(64, 128)
        tops, tots = [], []
        for j in range(count):
            tops.append(packed if j == 0 else pltpu.roll(packed, 128 - 32 * j, 1))
            tots.append(pltpu.roll(packed, 128 - 32 * j - TH, 1))
        ml = jnp.stack([t.reshape(8, 8, 128) for t in tops], axis=1).reshape(8, piece, 128)
        tot = jnp.stack([t.reshape(8, 8, 128) for t in tots], axis=1).reshape(8, piece, 128)
        real = iota((8, piece, 128), 2) < TH
        ml = jnp.where(real, ml, 0.0)
        tot = jnp.where(real, tot, 1.0)
        top = jnp.max(ml, axis=0, keepdims=True)
        factor = jnp.exp(ml - top)
        weight = factor / jnp.sum(factor * tot, axis=0, keepdims=True)
        weight = weight.reshape(8 * piece, 128)
        high = weight.astype(BF16)
        low = (weight - high.astype(F32)).astype(BF16)
        wide = (mm(high, expand) + mm(low, expand)).reshape(8, piece, CT)
        mix = jnp.sum(wide * rbuf[part][...].astype(F32), axis=0).astype(BF16)
        obuf[part][...] = (rep[owned(part, k), :].astype(F32) + mm(mix, wo[...])).astype(BF16)
        own = pltpu.make_async_copy(obuf[part], tout_h.at[owned(part, k)], osem.at[1 + part])
        own.start()
        for i in range(1, 8):
            peer = lax.rem(k + i, 8)
            copy = send(
                obuf[part], tout_h.at[owned(part, k)], gs.at[part, i], gr.at[part, i], p, peer
            )
            copy.start()
            gathers[part].append(copy)
        return own

    for n in range(len(CHUNKS[0])):
        attend(0, n)
    share_sums(0)
    attend(1, 0)
    own_a = merge(0)
    attend(1, 1)
    share_sums(1)
    own_b = merge(1)
    own_a.wait()
    own_b.wait()
    aout_copy.wait()
    for part in range(2):
        for i in range(1, 8):
            src = lax.rem(k + 8 - i, 8)
            send(
                obuf[part], tout_h.at[owned(part, src)], gs.at[part, i], gr.at[part, i], p, src
            ).wait_recv()
    for copy in gathers[0] + gathers[1] + sends[0] + sends[1] + fwds:
        copy.wait_send()

    @pl.when(outer)
    def _():
        for f in range(len(FEATURES)):
            for i in (2, 4, 6):
                directs[f][i - 1].wait_send()
            hops[f].wait_send()
            for copy in onward[f]:
                copy.wait_send()

    @pl.when(jnp.logical_not(outer))
    def _():
        for f in range(len(FEATURES)):
            for copy in directs[f]:
                copy.wait_send()

    @pl.when(p < last)
    def _():
        to_right.wait_send()
        ids_right.wait_send()
        tail_right.wait_send()

    @pl.when(p > 0)
    def _():
        to_left.wait_send()


def body(
    atoms,
    atom_gain,
    atom_qkv,
    atom_proj,
    atom_bias,
    window_shift,
    token_of_atom,
    agg_weight,
    token_gain,
    token_q,
    token_kv,
    token_o,
    pair_bias,
):
    hbm = pl.BlockSpec(memory_space=pl.ANY)
    vm = pltpu.VMEM
    dma = pltpu.SemaphoreType.DMA
    return pl.pallas_call(
        kernel,
        out_shape=(
            jax.ShapeDtypeStruct((AR, 128), BF16),
            jax.ShapeDtypeStruct((TR, CT), BF16),
        ),
        in_specs=[pl.BlockSpec(memory_space=pltpu.SMEM)] + [hbm] * 12,
        out_specs=(hbm, hbm),
        scratch_shapes=[
            vm((EXT, 128), BF16),
            vm((1, 128), F32),
            vm((128, 384), BF16),
            vm((128, 128), BF16),
            vm((4, AR, WK), BF16),
            vm((1, AR + TAIL), I32),
            vm((128, CT), BF16),
            vm((CT,), F32),
            vm((CT, CT), BF16),
            vm((CT, 2 * CT), BF16),
            vm((CT, CT), BF16),
            vm((TH, TR, 2 * TR), BF16),
            vm((AR, 128), BF16),
            vm((EXT, 128), F32),
            vm((EXT, 128), F32),
            vm((AR, 128), BF16),
            vm((AR + TAIL, 128), BF16),
            vm((TR, AR + TAIL), BF16),
            vm((AR + TAIL, 256), BF16),
            vm((PIECE, CT), BF16),
            vm((2 * TR, CT), BF16),
            vm((TR, CT), BF16),
            vm((TR, CT), BF16),
            vm((TR, CT), BF16),
            vm((2 * TR, CT), BF16),
            vm((2 * TR, CT), BF16),
            vm((2 * TR, CT), BF16),
            vm((TR, CT), F32),
            vm((TR, 128), F32),
            vm((TR, CT), BF16),
            vm((8, 32, CT), BF16),
            vm((8, 16, CT), BF16),
            vm((8, 8, 128), F32),
            vm((8, 8, 128), F32),
            vm((8, 8, 128), F32),
            vm((8, 8, 128), F32),
            vm((32, CT), BF16),
            vm((16, CT), BF16),
            dma((11,)),
            dma,
            dma((3,)),
            dma((4,)),
            dma((4,)),
            dma((3, 8)),
            dma((3, 8)),
            dma((3,)),
            dma((3,)),
            dma((3, 4)),
            dma((3,)),
            dma((3,)),
            dma((2, 4, 8)),
            dma((2, 4, 8)),
            dma((2, 8)),
            dma((2, 8)),
        ],
        compiler_params=pltpu.CompilerParams(
            collective_id=0, has_side_effects=True, vmem_limit_bytes=60 * 1024 * 1024
        ),
    )(
        window_shift,
        atoms,
        atom_gain.reshape(1, 128),
        atom_qkv,
        atom_proj,
        atom_bias,
        token_of_atom.reshape(1, AR),
        agg_weight,
        token_gain,
        token_q,
        token_kv,
        token_o,
        pair_bias,
    )


def solution(mesh):
    return jax.shard_map(
        body,
        mesh=mesh,
        in_specs=(
            P("pb", None),
            P(),
            P(),
            P(),
            P(None, "pb", None),
            P("pb"),
            P("pb"),
            P(),
            P(),
            P(),
            P(),
            P(),
            P(None, "pb", "ka"),
        ),
        out_specs=(P("pb", None), P("pb", None)),
        check_vma=False,
    )
```

```python
import functools
import math

import jax
import jax.numpy as jnp
from jax import lax
from jax.experimental import pallas as pl
from jax.experimental.pallas import tpu as pltpu
from jax.sharding import PartitionSpec as P

F32, BF16, I32 = jnp.float32, jnp.bfloat16, jnp.int32
AR, HALO, TAIL, WQ, WK = 3072, 64, 384, 32, 128
EXT = AR + 2 * HALO
TR, CT, TH, HD = 384, 768, 16, 48
PIECE = TR // 8
PARTS = ((0, 256), (256, 128))
WINDOWS = AR // WQ
UNROLL = 8
CHUNKS = (((0, 8, 0, 384), (8, 14, 384, 256), (14, 16, 640, 128)), ((0, 8, 0, 384), (8, 16, 384, 384)))
FEATURES = (0, 256, 512)
NT = (((1,), (1,)), ((), ()))
NN = (((1,), (0,)), ((), ()))


def iota(shape, dim):
    return lax.broadcasted_iota(I32, shape, dim)


def mm(a, b, dims=NN):
    return lax.dot_general(a, b, dims, preferred_element_type=F32)


def normed(x, gain):
    centre = jnp.mean(x, axis=-1, keepdims=True)
    diff = x - centre
    spread = jnp.mean(diff * diff, axis=-1, keepdims=True)
    return (diff * lax.rsqrt(spread + 1e-05) * gain).astype(BF16)


def kernel(
    shift_ref,
    atoms_h,
    again_h,
    qkv_h,
    proj_h,
    abias_h,
    ids_h,
    agg_h,
    tgain_h,
    wq_h,
    wkv_h,
    wo_h,
    pair_h,
    aout_h,
    tout_h,
    xs,
    again,
    wqkv,
    wproj,
    ab,
    ids,
    wagg,
    tgain,
    wq,
    wkv,
    wo,
    pbm,
    qs,
    kf,
    vf,
    ms,
    ao,
    hot,
    hid,
    rly,
    kn,
    rep,
    nrm,
    qt,
    kt,
    kk,
    vv,
    osc,
    mlb,
    mixb,
    rbuf_a,
    rbuf_b,
    mlp_a,
    mlp_b,
    rml_a,
    rml_b,
    obuf_a,
    obuf_b,
    lsem,
    psem,
    osem,
    hs,
    hr,
    xsem,
    xrsem,
    rls,
    rlr,
    rfs,
    fs,
    fr,
    rs,
    rr,
    gs,
    gr,
):
    rbuf, mlp, rml, obuf = (rbuf_a, rbuf_b), (mlp_a, mlp_b), (rml_a, rml_b), (obuf_a, obuf_b)
    p = lax.axis_index("pb")
    k = lax.axis_index("ka")
    c = lax.rem(p, 2)
    cp = lax.div(p, 2)
    zh, zl = lax.rem(cp, 2), lax.rem(k, 2)
    outer = zh == zl
    cp_flip, k_flip, p_flip = cp + 1 - 2 * zh, k + 1 - 2 * zl, p + 2 - 4 * zh
    last = 15
    barrier = pltpu.get_barrier_semaphore()

    def dev(pb, ka):
        return {"pb": pb, "ka": ka}

    def hello(pb, ka):
        pl.semaphore_signal(barrier, inc=1, device_id=dev(pb, ka), device_id_type=pl.DeviceIdType.MESH)

    def send(src, dst, ssem, rsem, pb, ka):
        return pltpu.make_async_remote_copy(
            src_ref=src,
            dst_ref=dst,
            send_sem=ssem,
            recv_sem=rsem,
            device_id=dev(pb, ka),
            device_id_type=pl.DeviceIdType.MESH,
        )

    copies = {}

    def load(name, src, dst, sem):
        copies[name] = pltpu.make_async_copy(src, dst, sem)
        copies[name].start()

    load("atoms", atoms_h, xs.at[pl.ds(HALO, AR)], lsem.at[0])
    load("again", again_h, again, lsem.at[1])
    load("qkv", qkv_h, wqkv, lsem.at[2])
    @pl.when(p > 0)
    def _():
        hello(p - 1, k)

    @pl.when(p < last)
    def _():
        hello(p + 1, k)

    for i in range(1, 8):
        hello(p, lax.rem(k + i, 8))

    def direct(i):
        return lax.rem(cp + i, 8) * 2 + c

    def relayed(x):
        return (2 * x + zh) * 2 + c

    @pl.when(outer)
    def _():
        for i in (2, 4, 6):
            hello(direct(i), cp)
        for x in range(4):
            hello(relayed(x), cp_flip)
        hello(p_flip, k_flip)

    @pl.when(jnp.logical_not(outer))
    def _():
        for i in range(1, 8):
            hello(direct(i), cp)
        for y in range(4):
            hello(2 * (k + 1 - 2 * zl) + c, 2 * y + 1 - zl)
            hello(2 * k + c, 2 * y + 1 - zl)

    @pl.when(jnp.logical_and(outer, k != cp))
    def _():
        for s in range(8):
            hello(2 * k + c, s)

    load("abias", abias_h, ab, lsem.at[3])
    load("proj", proj_h, wproj, lsem.at[4])
    load("agg", agg_h, wagg, lsem.at[5])
    load("ids", ids_h, ids.at[:, pl.ds(0, AR)], lsem.at[6])
    load("tgain", tgain_h, tgain, lsem.at[7])
    load("wq", wq_h, wq, lsem.at[8])
    load("wkv", wkv_h, wkv, lsem.at[9])
    load("wo", wo_h, wo, lsem.at[10])
    load("pair", pair_h, pbm, psem)

    scale = 1.0 / math.sqrt(32.0)

    def project(parts, rows, queries):
        outs = [
            mm(normed(xs[pl.ds(row, rows), :].astype(F32), again[...]), wqkv[...]) for row in parts
        ]
        for row, y in zip(parts, outs):
            if queries:
                qs[pl.ds(row - HALO, rows), :] = (y[:, 0:128] * scale).astype(BF16)
            kf[pl.ds(row, rows), :] = y[:, 128:256].astype(BF16).astype(F32)
            vf[pl.ds(row, rows), :] = y[:, 256:384].astype(BF16).astype(F32)

    copies["atoms"].wait()
    copies["again"].wait()
    copies["qkv"].wait()

    def project_own(i, carry):
        base = HALO + i * 768
        project([pl.multiple_of(base + u * 256, 64) for u in range(3)], 256, True)
        return carry

    lax.fori_loop(0, AR // 768, project_own, 0)

    copies["abias"].wait()
    copies["proj"].wait()

    head_mask = jnp.where(
        (iota((128, 128), 0) >> 5) == (iota((128, 128), 1) >> 5), 1.0, 0.0
    ).astype(BF16)
    lane_head = iota((WQ, 128), 1) >> 5
    ones = jnp.ones((WK, 128), BF16)

    def by_head(o):
        return jnp.where(
            lane_head == 0,
            o[0:32],
            jnp.where(lane_head == 1, o[32:64], jnp.where(lane_head == 2, o[64:96], o[96:128])),
        )

    def scores(b, masked):
        base = pl.multiple_of(b * WQ, WQ)
        first = base + jnp.clip(shift_ref[b], -HALO, WQ - HALO)
        kw = kf[pl.ds(first + HALO, WK), :].astype(BF16)
        q = qs[pl.ds(base, WQ), :]
        q4 = jnp.concatenate([q, q, q, q], axis=0) * head_mask
        s = mm(q4, kw, NT) + ab[:, pl.ds(base, WQ), :].reshape(128, WK).astype(F32)
        if masked:
            j = first + p * AR + iota((1, WK), 1)
            s = jnp.where((j >= 0) & (j < AR * 16), s, -1e30)
        return base, first, s

    def windows(lo, hi, masked):
        def group(g, carry):
            part = [scores(g * UNROLL + u, masked) for u in range(UNROLL)]
            tops = [jnp.max(s, axis=-1, keepdims=True) for _, _, s in part]
            weights = [jnp.exp(s - t).astype(BF16) for (_, _, s), t in zip(part, tops)]
            mixes = []
            for (_, first, _), w in zip(part, weights):
                vw = vf[pl.ds(first + HALO, WK), :].astype(BF16)
                mixes.append(mm(w, jnp.concatenate([vw, ones], axis=1)))
            for (base, _, _), o in zip(part, mixes):
                ms[pl.ds(base, WQ), :] = (
                    by_head(o[:, 0:128]) / by_head(o[:, 128:256])
                ).astype(BF16)
            return carry

        lax.fori_loop(lo // UNROLL, hi // UNROLL, group, 0)

    def finish_rows(row, rows):
        r = pl.ds(row, rows)
        y = xs[pl.ds(row + HALO, rows), :].astype(F32) + mm(ms[r, :], wproj[...])
        ao[r, :] = y.astype(BF16)

    def chunk(i):
        return i * 384 if isinstance(i, int) else pl.multiple_of(i * 384, 384)

    def hidden(f, parts):
        cols = pl.ds(FEATURES[f], 256)
        rows = [pl.ds(chunk(i), 384) for i in parts]
        outs = [mm(ao[r, :], wagg[:, cols]) for r in rows]
        for r, v in zip(rows, outs):
            hid[f, r, :] = (0.5 * v * (1.0 + jnp.tanh(0.5 * v))).astype(BF16)

    def hidden_three(f, lo, hi):
        def body(g, carry):
            hidden(f, [g * 3 + u for u in range(3)])
            return carry

        lax.fori_loop(lo, hi, body, 0)

    def finish(i, carry):
        finish_rows(chunk(i), 384)
        return carry

    def slots(row, rows):
        local = ids[:, pl.ds(row, rows)] - p * TR
        hits = jnp.where(local == iota((TR, rows), 0), 1.0, 0.0)
        hot[:, pl.ds(row, rows)] = hits.astype(BF16)
        mlb[...] += hits[:, 0:128] + hits[:, 128:256] + hits[:, 256:384]

    def slots_own(i, carry):
        slots(pl.multiple_of(i * 384, 128), 384)
        return carry

    windows(8, 32, False)

    greeted = (
        14
        + jnp.where(p > 0, 1, 0)
        + jnp.where(p < last, 1, 0)
        + jnp.where(k != cp, 8, 0)
        + jnp.where(outer, 1, 0)
    )
    pl.semaphore_wait(barrier, greeted)
    right = jnp.minimum(p + 1, last)
    left = jnp.maximum(p - 1, 0)
    to_right = send(
        atoms_h.at[pl.ds(AR - HALO, HALO)], xs.at[pl.ds(0, HALO)], hs.at[0], hr.at[0], right, k
    )
    to_left = send(
        atoms_h.at[pl.ds(0, HALO)], xs.at[pl.ds(HALO + AR, HALO)], hs.at[1], hr.at[1], left, k
    )
    ids_right = send(
        ids_h.at[:, pl.ds(AR - TAIL, TAIL)], ids.at[:, pl.ds(AR, TAIL)], hs.at[2], hr.at[2], right, k
    )
    tail_right = send(
        ao.at[pl.ds(AR - TAIL, TAIL)], ao.at[pl.ds(AR, TAIL)], hs.at[3], hr.at[3], right, k
    )

    @pl.when(p < last)
    def _():
        to_right.start()
        ids_right.start()

    @pl.when(p > 0)
    def _():
        to_left.start()

    windows(32, 80, False)
    copies["ids"].wait()
    mlb[...] = jnp.zeros((TR, 128), F32)
    lax.fori_loop(0, AR // 384, slots_own, 0)
    lax.fori_loop(1, 6, finish, 0)
    copies["agg"].wait()
    hidden(0, (1, 2, 3))
    hidden(0, (4, 5))

    @pl.when(p > 0)
    def _():
        to_right.wait_recv()

    @pl.when(p < last)
    def _():
        to_left.wait_recv()

    @pl.when(p == 0)
    def _():
        xs[pl.ds(0, HALO), :] = jnp.zeros((HALO, 128), BF16)

    @pl.when(p == last)
    def _():
        xs[pl.ds(HALO + AR, HALO), :] = jnp.zeros((HALO, 128), BF16)

    project([0, HALO + AR], HALO, False)
    windows(80, 96, True)
    finish_rows(AR - TAIL, TAIL)

    @pl.when(p < last)
    def _():
        tail_right.start()

    windows(0, 8, True)

    finish(0, 0)
    finish(6, 0)
    aout_copy = pltpu.make_async_copy(ao.at[pl.ds(0, AR)], aout_h, osem.at[0])
    aout_copy.start()

    copies["tgain"].wait()
    def tail_rows():
        @pl.when(p > 0)
        def _():
            ids_right.wait_recv()
            tail_right.wait_recv()

        @pl.when(p == 0)
        def _():
            ids[:, pl.ds(AR, TAIL)] = jnp.full((1, TAIL), -1, I32)
            ao[pl.ds(AR, TAIL), :] = jnp.zeros((TAIL, 128), BF16)

        slots(AR, TAIL)

    def rows48(i):
        return pl.ds(pl.multiple_of(i * PIECE, 16), PIECE)

    def landing(core, source):
        return pl.ds(pl.multiple_of(core * TR + source * PIECE, 16), PIECE)

    def half(i):
        return pl.ds(pl.multiple_of(i * TR, 16), TR)

    directs, hops, onward = [], [], []
    for f, col in enumerate(FEATURES):
        cols = pl.ds(col, 256)
        directs.append(
            [
                send(
                    rep.at[rows48(k), cols],
                    kt.at[landing(c, k), cols],
                    xsem.at[f, i],
                    xrsem.at[f, k],
                    direct(i),
                    cp,
                )
                for i in range(1, 8)
            ]
        )
        hops.append(
            send(rep.at[rows48(k), cols], rly.at[:, cols], rls.at[f], rlr.at[f], p_flip, k_flip)
        )
        onward.append(
            [
                send(
                    rly.at[:, cols],
                    kt.at[landing(c, k_flip), cols],
                    rfs.at[f, x],
                    xrsem.at[f, k_flip],
                    relayed(x),
                    cp_flip,
                )
                for x in range(4)
            ]
        )

    def pass_on(f):
        @pl.when(outer)
        def _():
            hops[f].wait_recv()
            for copy in onward[f]:
                copy.start()

    for f, col in enumerate(FEATURES):
        cols = pl.ds(col, 256)

        if f == 0:
            hidden(0, (0, 6, 7))
            pooled = mm(hot[:, 0:AR], hid[0, 0:AR, :])
            hidden_three(1, 0, 2)
            hidden(1, (6, 7))
            tail_rows()
            hidden(0, (8,))
            hidden(1, (8,))
            counts = jnp.sum(mlb[...], axis=1, keepdims=True)
            pooled += mm(hot[:, AR : AR + TAIL], hid[0, AR : AR + TAIL, :])
        else:
            if f == 2:
                hidden_three(2, 0, 3)
            pooled = mm(hot[...], hid[f])
        rep[:, cols] = (pooled / counts).astype(BF16)

        @pl.when(outer)
        def _():
            for i in (2, 4, 6):
                directs[f][i - 1].start()
            hops[f].start()

        @pl.when(jnp.logical_not(outer))
        def _():
            for copy in directs[f]:
                copy.start()

        if f > 0:
            pass_on(f - 1)

    tscale = 1.0 / math.sqrt(float(HD))
    copies["wq"].wait()
    nrm[...] = normed(rep[...].astype(F32), tgain[...].reshape(1, CT))
    qt[...] = (mm(nrm[...], wq[...]) * tscale).astype(BF16)
    pass_on(len(FEATURES) - 1)
    partner = p + 1 - 2 * c

    @pl.when(k == cp)
    def _():
        kt[half(c), :] = rep[...]

    fwds, backs = [], []
    for f, col in enumerate(FEATURES):
        cols = pl.ds(col, 256)
        fwds.append(
            send(kt.at[half(c), cols], kt.at[half(c), cols], fs.at[f], fr.at[f], partner, k)
        )
        backs.append(
            send(kt.at[half(c), cols], kt.at[half(1 - c), cols], fs.at[f], fr.at[f], partner, k)
        )

        @pl.when(k != cp)
        def _():
            for s in range(8):
                send(
                    rep.at[rows48(0), cols],
                    kt.at[landing(c, s), cols],
                    xsem.at[f, 0],
                    xrsem.at[f, s],
                    partner,
                    k,
                ).wait_recv()

        fwds[f].start()

    def project_half(i):
        r = half(i)
        kn[...] = normed(kt[r, :].astype(F32), tgain[...].reshape(1, CT))

        def keyvals(j, carry):
            cols = pl.ds(pl.multiple_of(j * 256, 256), 256)
            kk[r, cols] = mm(kn[...], wkv[:, cols]).astype(BF16)
            vcols = pl.ds(pl.multiple_of(j * 256 + CT, 256), 256)
            vv[r, cols] = mm(kn[...], wkv[:, vcols]).astype(BF16)
            return carry

        lax.fori_loop(0, CT // 256, keyvals, 0)

    copies["wkv"].wait()
    project_half(c)
    for copy in backs:
        copy.wait_recv()
    project_half(1 - c)
    copies["pair"].wait()
    rb = 128
    l128 = iota((rb, 128), 1)
    copies["wo"].wait()

    def make_heads(row, rows, together):
        def heads(group, carry):
            work = []
            for u in range(together):
                h = group * together + u
                lane0 = pl.multiple_of(jnp.minimum(lax.div(h * HD, 128), 4) * 128, 128)
                off = h * HD - lane0
                lanes = pl.ds(lane0, 256)
                lane = iota((1, 256), 1)
                mask = (lane >= off) & (lane < off + HD)
                keep = jnp.where(mask, 1.0, 0.0).astype(BF16)
                values = vv[:, lanes] * keep + (1.0 - keep)
                for r in range(row, row + rows, rb):
                    work.append((h, lanes, mask, keep, values, pl.ds(r, rb)))

            def score(h, lanes, mask, keep, values, r):
                return mm(qt[r, lanes] * keep, kk[:, lanes], NT) + pbm[h, r, :].astype(F32)

            def store(h, lanes, mask, r, top, o):
                osc[r, lanes] = jnp.where(mask, o, osc[r, lanes])
                total = jnp.where(mask[:, 0:128], o[:, 128:256], o[:, 0:128])
                mlb[r, :] = jnp.where(l128 == h, top, jnp.where(l128 == h + TH, total, mlb[r, :]))

            ahead = score(*work[0])
            done = None
            for n, (h, lanes, mask, keep, values, r) in enumerate(work):
                s = ahead
                if n + 1 < len(work):
                    ahead = score(*work[n + 1])
                top = jnp.max(s, axis=-1, keepdims=True)
                o = mm(jnp.exp(s - top).astype(BF16), values)
                if done is not None:
                    store(*done)
                done = (h, lanes, mask, r, top, o)
            store(*done)
            return carry

        return heads

    i0, j0 = iota((128, CT), 0) * HD, iota((128, CT), 1)
    expand = jnp.where((j0 >= i0) & (j0 < i0 + HD), 1.0, 0.0).astype(BF16)
    sends, gathers = ([], []), ([], [])

    def owned(part, owner):
        row, rows = PARTS[part]
        return pl.ds(pl.multiple_of(row + owner * (rows // 8), 16), rows // 8)

    def attend(part, n):
        row, rows = PARTS[part]
        lo, hi, col, width = CHUNKS[part][n]
        together = 512 // rows
        lax.fori_loop(lo // together, hi // together, make_heads(row, rows, together), 0)
        cols = pl.ds(col, width)
        mixb[pl.ds(row, rows), cols] = osc[pl.ds(row, rows), cols].astype(BF16)
        for i in range(1, 8):
            peer = lax.rem(k + i, 8)
            copy = send(
                mixb.at[owned(part, peer), cols],
                rbuf[part].at[i, :, cols],
                rs.at[part, n, i],
                rr.at[part, n, i],
                p,
                peer,
            )
            copy.start()
            sends[part].append(copy)

    def share_sums(part):
        row, rows = PARTS[part]
        count = rows // 64
        grouped = mlb[pl.ds(row, rows), :].reshape(8, count, 8, 128)
        lane = iota((8, 8, 128), 2)
        packed = grouped[:, 0]
        for j in range(1, count):
            turned = pltpu.roll(grouped[:, j].reshape(64, 128), 32 * j, 1).reshape(8, 8, 128)
            packed = jnp.where(lane >= 32 * j, turned, packed)
        mlp[part][...] = packed
        for i in range(1, 8):
            peer = lax.rem(k + i, 8)
            copy = send(
                mlp[part].at[peer], rml[part].at[i], rs.at[part, 3, i], rr.at[part, 3, i], p, peer
            )
            copy.start()
            sends[part].append(copy)

    def merge(part):
        row, rows = PARTS[part]
        piece, count = rows // 8, rows // 64
        rbuf[part][0, :, :] = mixb[owned(part, k), :]
        rml[part][0, :, :] = mlp[part][k, :, :]
        for copy in sends[part]:
            copy.wait_recv()
        packed = rml[part][...].reshape(64, 128)
        tops, tots = [], []
        for j in range(count):
            tops.append(packed if j == 0 else pltpu.roll(packed, 128 - 32 * j, 1))
            tots.append(pltpu.roll(packed, 128 - 32 * j - TH, 1))
        ml = jnp.stack([t.reshape(8, 8, 128) for t in tops], axis=1).reshape(8, piece, 128)
        tot = jnp.stack([t.reshape(8, 8, 128) for t in tots], axis=1).reshape(8, piece, 128)
        real = iota((8, piece, 128), 2) < TH
        ml = jnp.where(real, ml, 0.0)
        tot = jnp.where(real, tot, 1.0)
        top = jnp.max(ml, axis=0, keepdims=True)
        factor = jnp.exp(ml - top)
        weight = factor / jnp.sum(factor * tot, axis=0, keepdims=True)
        weight = weight.reshape(8 * piece, 128)
        high = weight.astype(BF16)
        low = (weight - high.astype(F32)).astype(BF16)
        wide = (mm(high, expand) + mm(low, expand)).reshape(8, piece, CT)
        mix = jnp.sum(wide * rbuf[part][...].astype(F32), axis=0).astype(BF16)
        obuf[part][...] = (rep[owned(part, k), :].astype(F32) + mm(mix, wo[...])).astype(BF16)
        own = pltpu.make_async_copy(obuf[part], tout_h.at[owned(part, k)], osem.at[1 + part])
        own.start()
        for i in range(1, 8):
            peer = lax.rem(k + i, 8)
            copy = send(
                obuf[part], tout_h.at[owned(part, k)], gs.at[part, i], gr.at[part, i], p, peer
            )
            copy.start()
            gathers[part].append(copy)
        return own

    for n in range(len(CHUNKS[0])):
        attend(0, n)
    share_sums(0)
    attend(1, 0)
    attend(1, 1)
    share_sums(1)
    own_a = merge(0)
    own_b = merge(1)
    own_a.wait()
    own_b.wait()
    aout_copy.wait()
    for part in range(2):
        for i in range(1, 8):
            src = lax.rem(k + 8 - i, 8)
            send(
                obuf[part], tout_h.at[owned(part, src)], gs.at[part, i], gr.at[part, i], p, src
            ).wait_recv()
    for copy in gathers[0] + gathers[1] + sends[0] + sends[1] + fwds:
        copy.wait_send()

    @pl.when(outer)
    def _():
        for f in range(len(FEATURES)):
            for i in (2, 4, 6):
                directs[f][i - 1].wait_send()
            hops[f].wait_send()
            for copy in onward[f]:
                copy.wait_send()

    @pl.when(jnp.logical_not(outer))
    def _():
        for f in range(len(FEATURES)):
            for copy in directs[f]:
                copy.wait_send()

    @pl.when(p < last)
    def _():
        to_right.wait_send()
        ids_right.wait_send()
        tail_right.wait_send()

    @pl.when(p > 0)
    def _():
        to_left.wait_send()


def body(
    atoms,
    atom_gain,
    atom_qkv,
    atom_proj,
    atom_bias,
    window_shift,
    token_of_atom,
    agg_weight,
    token_gain,
    token_q,
    token_kv,
    token_o,
    pair_bias,
):
    hbm = pl.BlockSpec(memory_space=pl.ANY)
    vm = pltpu.VMEM
    dma = pltpu.SemaphoreType.DMA
    return pl.pallas_call(
        kernel,
        out_shape=(
            jax.ShapeDtypeStruct((AR, 128), BF16),
            jax.ShapeDtypeStruct((TR, CT), BF16),
        ),
        in_specs=[pl.BlockSpec(memory_space=pltpu.SMEM)] + [hbm] * 12,
        out_specs=(hbm, hbm),
        scratch_shapes=[
            vm((EXT, 128), BF16),
            vm((1, 128), F32),
            vm((128, 384), BF16),
            vm((128, 128), BF16),
            vm((4, AR, WK), BF16),
            vm((1, AR + TAIL), I32),
            vm((128, CT), BF16),
            vm((CT,), F32),
            vm((CT, CT), BF16),
            vm((CT, 2 * CT), BF16),
            vm((CT, CT), BF16),
            vm((TH, TR, 2 * TR), BF16),
            vm((AR, 128), BF16),
            vm((EXT, 128), F32),
            vm((EXT, 128), F32),
            vm((AR, 128), BF16),
            vm((AR + TAIL, 128), BF16),
            vm((TR, AR + TAIL), BF16),
            vm((3, AR + TAIL, 256), BF16),
            vm((PIECE, CT), BF16),
            vm((TR, CT), BF16),
            vm((TR, CT), BF16),
            vm((TR, CT), BF16),
            vm((TR, CT), BF16),
            vm((2 * TR, CT), BF16),
            vm((2 * TR, CT), BF16),
            vm((2 * TR, CT), BF16),
            vm((TR, CT), F32),
            vm((TR, 128), F32),
            vm((TR, CT), BF16),
            vm((8, 32, CT), BF16),
            vm((8, 16, CT), BF16),
            vm((8, 8, 128), F32),
            vm((8, 8, 128), F32),
            vm((8, 8, 128), F32),
            vm((8, 8, 128), F32),
            vm((32, CT), BF16),
            vm((16, CT), BF16),
            dma((11,)),
            dma,
            dma((3,)),
            dma((4,)),
            dma((4,)),
            dma((3, 8)),
            dma((3, 8)),
            dma((3,)),
            dma((3,)),
            dma((3, 4)),
            dma((3,)),
            dma((3,)),
            dma((2, 4, 8)),
            dma((2, 4, 8)),
            dma((2, 8)),
            dma((2, 8)),
        ],
        compiler_params=pltpu.CompilerParams(
            collective_id=0, has_side_effects=True, vmem_limit_bytes=60 * 1024 * 1024
        ),
    )(
        window_shift,
        atoms,
        atom_gain.reshape(1, 128),
        atom_qkv,
        atom_proj,
        atom_bias,
        token_of_atom.reshape(1, AR),
        agg_weight,
        token_gain,
        token_q,
        token_kv,
        token_o,
        pair_bias,
    )


def solution(mesh):
    return jax.shard_map(
        body,
        mesh=mesh,
        in_specs=(
            P("pb", None),
            P(),
            P(),
            P(),
            P(None, "pb", None),
            P("pb"),
            P("pb"),
            P(),
            P(),
            P(),
            P(),
            P(),
            P(None, "pb", "ka"),
        ),
        out_specs=(P("pb", None), P("pb", None)),
        check_vma=False,
    )
```

```python
import functools
import math

import jax
import jax.numpy as jnp
from jax import lax
from jax.experimental import pallas as pl
from jax.experimental.pallas import tpu as pltpu
from jax.sharding import PartitionSpec as P

F32, BF16, I32 = jnp.float32, jnp.bfloat16, jnp.int32
AR, HALO, TAIL, WQ, WK = 3072, 64, 384, 32, 128
EXT = AR + 2 * HALO
TR, CT, TH, HD = 384, 768, 16, 48
PIECE = TR // 8
PARTS = ((0, 256), (256, 128))
WINDOWS = AR // WQ
UNROLL = 8
CHUNKS = (((0, 8, 0, 384), (8, 14, 384, 256), (14, 16, 640, 128)), ((0, 8, 0, 384), (8, 16, 384, 384)))
FEATURES = (0, 256, 512)
NT = (((1,), (1,)), ((), ()))
NN = (((1,), (0,)), ((), ()))


def iota(shape, dim):
    return lax.broadcasted_iota(I32, shape, dim)


def mm(a, b, dims=NN):
    return lax.dot_general(a, b, dims, preferred_element_type=F32)


def normed(x, gain):
    centre = jnp.mean(x, axis=-1, keepdims=True)
    diff = x - centre
    spread = jnp.mean(diff * diff, axis=-1, keepdims=True)
    return (diff * lax.rsqrt(spread + 1e-05) * gain).astype(BF16)


def kernel(
    shift_ref,
    atoms_h,
    again_h,
    qkv_h,
    proj_h,
    abias_h,
    ids_h,
    agg_h,
    tgain_h,
    wq_h,
    wkv_h,
    wo_h,
    pair_h,
    aout_h,
    tout_h,
    xs,
    again,
    wqkv,
    wproj,
    ab,
    ids,
    wagg,
    tgain,
    wq,
    wkv,
    wo,
    pbm,
    qs,
    kf,
    vf,
    ms,
    ao,
    hot,
    hid,
    kn,
    rep,
    nrm,
    qt,
    kt,
    kk,
    vv,
    osc,
    mlb,
    mixb,
    rbuf_a,
    rbuf_b,
    mlp_a,
    mlp_b,
    rml_a,
    rml_b,
    obuf_a,
    obuf_b,
    lsem,
    psem,
    osem,
    hs,
    hr,
    xsem,
    xrsem,
    fs,
    fr,
    rs,
    rr,
    gs,
    gr,
):
    rbuf, mlp, rml, obuf = (rbuf_a, rbuf_b), (mlp_a, mlp_b), (rml_a, rml_b), (obuf_a, obuf_b)
    p = lax.axis_index("pb")
    k = lax.axis_index("ka")
    c = lax.rem(p, 2)
    cp = lax.div(p, 2)
    last = 15
    barrier = pltpu.get_barrier_semaphore()

    def dev(pb, ka):
        return {"pb": pb, "ka": ka}

    def hello(pb, ka):
        pl.semaphore_signal(barrier, inc=1, device_id=dev(pb, ka), device_id_type=pl.DeviceIdType.MESH)

    def send(src, dst, ssem, rsem, pb, ka):
        return pltpu.make_async_remote_copy(
            src_ref=src,
            dst_ref=dst,
            send_sem=ssem,
            recv_sem=rsem,
            device_id=dev(pb, ka),
            device_id_type=pl.DeviceIdType.MESH,
        )

    copies = {}

    def load(name, src, dst, sem):
        copies[name] = pltpu.make_async_copy(src, dst, sem)
        copies[name].start()

    load("atoms", atoms_h, xs.at[pl.ds(HALO, AR)], lsem.at[0])
    load("again", again_h, again, lsem.at[1])
    load("qkv", qkv_h, wqkv, lsem.at[2])
    @pl.when(p > 0)
    def _():
        hello(p - 1, k)

    @pl.when(p < last)
    def _():
        hello(p + 1, k)

    def direct(i):
        return lax.rem(cp + i, 8) * 2 + c

    for i in range(1, 8):
        hello(p, lax.rem(k + i, 8))
        hello(direct(i), cp)

    @pl.when(k != cp)
    def _():
        for s in range(8):
            hello(2 * k + c, s)

    load("abias", abias_h, ab, lsem.at[3])
    load("proj", proj_h, wproj, lsem.at[4])
    load("agg", agg_h, wagg, lsem.at[5])
    load("ids", ids_h, ids.at[:, pl.ds(0, AR)], lsem.at[6])
    load("tgain", tgain_h, tgain, lsem.at[7])
    load("wq", wq_h, wq, lsem.at[8])
    load("wkv", wkv_h, wkv, lsem.at[9])
    load("wo", wo_h, wo, lsem.at[10])
    load("pair", pair_h, pbm, psem)

    scale = 1.0 / math.sqrt(32.0)

    def project(parts, rows, queries):
        outs = [
            mm(normed(xs[pl.ds(row, rows), :].astype(F32), again[...]), wqkv[...]) for row in parts
        ]
        for row, y in zip(parts, outs):
            if queries:
                qs[pl.ds(row - HALO, rows), :] = (y[:, 0:128] * scale).astype(BF16)
            kf[pl.ds(row, rows), :] = y[:, 128:256].astype(BF16).astype(F32)
            vf[pl.ds(row, rows), :] = y[:, 256:384].astype(BF16).astype(F32)

    copies["atoms"].wait()
    copies["again"].wait()
    copies["qkv"].wait()

    def project_own(i, carry):
        base = HALO + i * 768
        project([pl.multiple_of(base + u * 256, 64) for u in range(3)], 256, True)
        return carry

    lax.fori_loop(0, AR // 768, project_own, 0)

    copies["abias"].wait()
    copies["proj"].wait()

    head_mask = jnp.where(
        (iota((128, 128), 0) >> 5) == (iota((128, 128), 1) >> 5), 1.0, 0.0
    ).astype(BF16)
    lane_head = iota((WQ, 128), 1) >> 5
    ones = jnp.ones((WK, 128), BF16)

    def by_head(o):
        return jnp.where(
            lane_head == 0,
            o[0:32],
            jnp.where(lane_head == 1, o[32:64], jnp.where(lane_head == 2, o[64:96], o[96:128])),
        )

    def scores(b, masked):
        base = pl.multiple_of(b * WQ, WQ)
        first = base + jnp.clip(shift_ref[b], -HALO, WQ - HALO)
        kw = kf[pl.ds(first + HALO, WK), :].astype(BF16)
        q = qs[pl.ds(base, WQ), :]
        q4 = jnp.concatenate([q, q, q, q], axis=0) * head_mask
        s = mm(q4, kw, NT) + ab[:, pl.ds(base, WQ), :].reshape(128, WK).astype(F32)
        if masked:
            j = first + p * AR + iota((1, WK), 1)
            s = jnp.where((j >= 0) & (j < AR * 16), s, -1e30)
        return base, first, s

    def windows(lo, hi, masked):
        def group(g, carry):
            part = [scores(g * UNROLL + u, masked) for u in range(UNROLL)]
            tops = [jnp.max(s, axis=-1, keepdims=True) for _, _, s in part]
            weights = [jnp.exp(s - t).astype(BF16) for (_, _, s), t in zip(part, tops)]
            mixes = []
            for (_, first, _), w in zip(part, weights):
                vw = vf[pl.ds(first + HALO, WK), :].astype(BF16)
                mixes.append(mm(w, jnp.concatenate([vw, ones], axis=1)))
            for (base, _, _), o in zip(part, mixes):
                ms[pl.ds(base, WQ), :] = (
                    by_head(o[:, 0:128]) / by_head(o[:, 128:256])
                ).astype(BF16)
            return carry

        lax.fori_loop(lo // UNROLL, hi // UNROLL, group, 0)

    def finish_rows(row, rows):
        r = pl.ds(row, rows)
        y = xs[pl.ds(row + HALO, rows), :].astype(F32) + mm(ms[r, :], wproj[...])
        ao[r, :] = y.astype(BF16)

    def chunk(i):
        return i * 384 if isinstance(i, int) else pl.multiple_of(i * 384, 384)

    def hidden(f, parts):
        cols = pl.ds(FEATURES[f], 256)
        rows = [pl.ds(chunk(i), 384) for i in parts]
        outs = [mm(ao[r, :], wagg[:, cols]) for r in rows]
        for r, v in zip(rows, outs):
            hid[f, r, :] = (0.5 * v * (1.0 + jnp.tanh(0.5 * v))).astype(BF16)

    def hidden_three(f, lo, hi):
        def body(g, carry):
            hidden(f, [g * 3 + u for u in range(3)])
            return carry

        lax.fori_loop(lo, hi, body, 0)

    def finish(i, carry):
        finish_rows(chunk(i), 384)
        return carry

    def slots(row, rows):
        local = ids[:, pl.ds(row, rows)] - p * TR
        hits = jnp.where(local == iota((TR, rows), 0), 1.0, 0.0)
        hot[:, pl.ds(row, rows)] = hits.astype(BF16)
        mlb[...] += hits[:, 0:128] + hits[:, 128:256] + hits[:, 256:384]

    def slots_own(i, carry):
        slots(pl.multiple_of(i * 384, 128), 384)
        return carry

    windows(8, 16, False)

    greeted = (
        14
        + jnp.where(p > 0, 1, 0)
        + jnp.where(p < last, 1, 0)
        + jnp.where(k != cp, 8, 0)
    )
    pl.semaphore_wait(barrier, greeted)
    right = jnp.minimum(p + 1, last)
    left = jnp.maximum(p - 1, 0)
    to_right = send(
        atoms_h.at[pl.ds(AR - HALO, HALO)], xs.at[pl.ds(0, HALO)], hs.at[0], hr.at[0], right, k
    )
    to_left = send(
        atoms_h.at[pl.ds(0, HALO)], xs.at[pl.ds(HALO + AR, HALO)], hs.at[1], hr.at[1], left, k
    )
    ids_right = send(
        ids_h.at[:, pl.ds(AR - TAIL, TAIL)], ids.at[:, pl.ds(AR, TAIL)], hs.at[2], hr.at[2], right, k
    )
    tail_right = send(
        ao.at[pl.ds(AR - TAIL, TAIL)], ao.at[pl.ds(AR, TAIL)], hs.at[3], hr.at[3], right, k
    )

    @pl.when(p < last)
    def _():
        to_right.start()
        ids_right.start()

    @pl.when(p > 0)
    def _():
        to_left.start()

    windows(16, 80, False)
    copies["ids"].wait()
    mlb[...] = jnp.zeros((TR, 128), F32)
    lax.fori_loop(0, AR // 384, slots_own, 0)

    @pl.when(p > 0)
    def _():
        to_right.wait_recv()

    @pl.when(p < last)
    def _():
        to_left.wait_recv()

    @pl.when(p == 0)
    def _():
        xs[pl.ds(0, HALO), :] = jnp.zeros((HALO, 128), BF16)

    @pl.when(p == last)
    def _():
        xs[pl.ds(HALO + AR, HALO), :] = jnp.zeros((HALO, 128), BF16)

    project([0, HALO + AR], HALO, False)
    windows(80, 96, True)
    finish_rows(AR - TAIL, TAIL)

    @pl.when(p < last)
    def _():
        tail_right.start()

    lax.fori_loop(1, 6, finish, 0)
    copies["agg"].wait()
    hidden(0, (1, 2, 3))
    hidden(0, (4, 5))
    windows(0, 8, True)

    finish(0, 0)
    finish(6, 0)
    aout_copy = pltpu.make_async_copy(ao.at[pl.ds(0, AR)], aout_h, osem.at[0])
    aout_copy.start()

    copies["tgain"].wait()
    def tail_rows():
        @pl.when(p > 0)
        def _():
            ids_right.wait_recv()
            tail_right.wait_recv()

        @pl.when(p == 0)
        def _():
            ids[:, pl.ds(AR, TAIL)] = jnp.full((1, TAIL), -1, I32)
            ao[pl.ds(AR, TAIL), :] = jnp.zeros((TAIL, 128), BF16)

        slots(AR, TAIL)

    def rows48(i):
        return pl.ds(pl.multiple_of(i * PIECE, 16), PIECE)

    def landing(core, source):
        return pl.ds(pl.multiple_of(core * TR + source * PIECE, 16), PIECE)

    def half(i):
        return pl.ds(pl.multiple_of(i * TR, 16), TR)

    def pooled_sends(f):
        cols = pl.ds(FEATURES[f], 256)
        for i in range(1, 8):
            send(
                rep.at[rows48(k), cols],
                kt.at[landing(c, k), cols],
                xsem.at[f],
                xrsem.at[f],
                direct(i),
                cp,
            ).start()

    for f, col in enumerate(FEATURES):
        cols = pl.ds(col, 256)

        if f == 0:
            hidden(0, (0, 6, 7))
            pooled = mm(hot[:, 0:AR], hid[0, 0:AR, :])
            hidden_three(1, 0, 2)
            hidden(1, (6, 7))
            tail_rows()
            hidden(0, (8,))
            hidden(1, (8,))
            counts = jnp.sum(mlb[...], axis=1, keepdims=True)
            pooled += mm(hot[:, AR : AR + TAIL], hid[0, AR : AR + TAIL, :])
        else:
            if f == 2:
                hidden_three(2, 0, 3)
            pooled = mm(hot[...], hid[f])
        rep[:, cols] = (pooled / counts).astype(BF16)

        pooled_sends(f)

    tscale = 1.0 / math.sqrt(float(HD))
    copies["wq"].wait()
    nrm[...] = normed(rep[...].astype(F32), tgain[...].reshape(1, CT))
    qt[...] = (mm(nrm[...], wq[...]) * tscale).astype(BF16)
    partner = p + 1 - 2 * c

    @pl.when(k == cp)
    def _():
        kt[half(c), :] = rep[...]

    fwds, backs = [], []
    for f, col in enumerate(FEATURES):
        cols = pl.ds(col, 256)
        fwds.append(
            send(kt.at[half(c), cols], kt.at[half(c), cols], fs.at[f], fr.at[f], partner, k)
        )
        backs.append(
            send(kt.at[half(c), cols], kt.at[half(1 - c), cols], fs.at[f], fr.at[f], partner, k)
        )

        @pl.when(k != cp)
        def _():
            send(
                kt.at[half(c), cols], kt.at[half(c), cols], xsem.at[f], xrsem.at[f], partner, k
            ).wait_recv()

        fwds[f].start()

    def project_half(i):
        r = half(i)
        kn[...] = normed(kt[r, :].astype(F32), tgain[...].reshape(1, CT))

        def keyvals(j, carry):
            cols = pl.ds(pl.multiple_of(j * 256, 256), 256)
            kk[r, cols] = mm(kn[...], wkv[:, cols]).astype(BF16)
            vcols = pl.ds(pl.multiple_of(j * 256 + CT, 256), 256)
            vv[r, cols] = mm(kn[...], wkv[:, vcols]).astype(BF16)
            return carry

        lax.fori_loop(0, CT // 256, keyvals, 0)

    copies["wkv"].wait()
    project_half(c)
    for copy in backs:
        copy.wait_recv()
    project_half(1 - c)
    copies["pair"].wait()
    rb = 128
    l128 = iota((rb, 128), 1)
    copies["wo"].wait()

    def make_heads(row, rows, together):
        def heads(group, carry):
            work = []
            for u in range(together):
                h = group * together + u
                lane0 = pl.multiple_of(jnp.minimum(lax.div(h * HD, 128), 4) * 128, 128)
                off = h * HD - lane0
                lanes = pl.ds(lane0, 256)
                lane = iota((1, 256), 1)
                mask = (lane >= off) & (lane < off + HD)
                keep = jnp.where(mask, 1.0, 0.0).astype(BF16)
                values = vv[:, lanes] * keep + (1.0 - keep)
                for r in range(row, row + rows, rb):
                    work.append((h, lanes, mask, keep, values, pl.ds(r, rb)))

            def score(h, lanes, mask, keep, values, r):
                return mm(qt[r, lanes] * keep, kk[:, lanes], NT) + pbm[h, r, :].astype(F32)

            def store(h, lanes, mask, r, top, o):
                osc[r, lanes] = jnp.where(mask, o, osc[r, lanes])
                total = jnp.where(mask[:, 0:128], o[:, 128:256], o[:, 0:128])
                mlb[r, :] = jnp.where(l128 == h, top, jnp.where(l128 == h + TH, total, mlb[r, :]))

            ahead = score(*work[0])
            done = None
            for n, (h, lanes, mask, keep, values, r) in enumerate(work):
                s = ahead
                if n + 1 < len(work):
                    ahead = score(*work[n + 1])
                top = jnp.max(s, axis=-1, keepdims=True)
                o = mm(jnp.exp(s - top).astype(BF16), values)
                if done is not None:
                    store(*done)
                done = (h, lanes, mask, r, top, o)
            store(*done)
            return carry

        return heads

    i0, j0 = iota((128, CT), 0) * HD, iota((128, CT), 1)
    expand = jnp.where((j0 >= i0) & (j0 < i0 + HD), 1.0, 0.0).astype(BF16)
    sends, gathers = ([], []), ([], [])

    def owned(part, owner):
        row, rows = PARTS[part]
        return pl.ds(pl.multiple_of(row + owner * (rows // 8), 16), rows // 8)

    def attend(part, n):
        row, rows = PARTS[part]
        lo, hi, col, width = CHUNKS[part][n]
        together = 512 // rows
        lax.fori_loop(lo // together, hi // together, make_heads(row, rows, together), 0)
        cols = pl.ds(col, width)
        mixb[pl.ds(row, rows), cols] = osc[pl.ds(row, rows), cols].astype(BF16)
        for i in range(1, 8):
            peer = lax.rem(k + i, 8)
            copy = send(
                mixb.at[owned(part, peer), cols],
                rbuf[part].at[i, :, cols],
                rs.at[part, n],
                rr.at[part, n],
                p,
                peer,
            )
            copy.start()
        every = rbuf[part].at[pl.ds(1, 7), :, cols]
        sends[part].append(send(every, every, rs.at[part, n], rr.at[part, n], p, lax.rem(k + 1, 8)))

    def share_sums(part):
        row, rows = PARTS[part]
        count = rows // 64
        grouped = mlb[pl.ds(row, rows), :].reshape(8, count, 8, 128)
        lane = iota((8, 8, 128), 2)
        packed = grouped[:, 0]
        for j in range(1, count):
            turned = pltpu.roll(grouped[:, j].reshape(64, 128), 32 * j, 1).reshape(8, 8, 128)
            packed = jnp.where(lane >= 32 * j, turned, packed)
        mlp[part][...] = packed
        for i in range(1, 8):
            peer = lax.rem(k + i, 8)
            copy = send(
                mlp[part].at[peer], rml[part].at[i], rs.at[part, 3], rr.at[part, 3], p, peer
            )
            copy.start()
        every = rml[part].at[pl.ds(1, 7)]
        sends[part].append(send(every, every, rs.at[part, 3], rr.at[part, 3], p, lax.rem(k + 1, 8)))

    def merge(part):
        row, rows = PARTS[part]
        piece, count = rows // 8, rows // 64
        rbuf[part][0, :, :] = mixb[owned(part, k), :]
        rml[part][0, :, :] = mlp[part][k, :, :]
        for copy in sends[part]:
            copy.wait_recv()
        packed = rml[part][...].reshape(64, 128)
        tops, tots = [], []
        for j in range(count):
            tops.append(packed if j == 0 else pltpu.roll(packed, 128 - 32 * j, 1))
            tots.append(pltpu.roll(packed, 128 - 32 * j - TH, 1))
        ml = jnp.stack([t.reshape(8, 8, 128) for t in tops], axis=1).reshape(8, piece, 128)
        tot = jnp.stack([t.reshape(8, 8, 128) for t in tots], axis=1).reshape(8, piece, 128)
        real = iota((8, piece, 128), 2) < TH
        ml = jnp.where(real, ml, 0.0)
        tot = jnp.where(real, tot, 1.0)
        top = jnp.max(ml, axis=0, keepdims=True)
        factor = jnp.exp(ml - top)
        weight = factor / jnp.sum(factor * tot, axis=0, keepdims=True)
        weight = weight.reshape(8 * piece, 128)
        high = weight.astype(BF16)
        low = (weight - high.astype(F32)).astype(BF16)
        wide = (mm(high, expand) + mm(low, expand)).reshape(8, piece, CT)
        mix = jnp.sum(wide * rbuf[part][...].astype(F32), axis=0).astype(BF16)
        obuf[part][...] = (rep[owned(part, k), :].astype(F32) + mm(mix, wo[...])).astype(BF16)
        own = pltpu.make_async_copy(obuf[part], tout_h.at[owned(part, k)], osem.at[1 + part])
        own.start()
        for i in range(1, 8):
            peer = lax.rem(k + i, 8)
            copy = send(
                obuf[part], tout_h.at[owned(part, k)], gs.at[part], gr.at[part], p, peer
            )
            copy.start()
        every = tout_h.at[pl.ds(row, 7 * piece)]
        gathers[part].append(send(every, every, gs.at[part], gr.at[part], p, lax.rem(k + 1, 8)))
        return own

    for n in range(len(CHUNKS[0])):
        attend(0, n)
    share_sums(0)
    attend(1, 0)
    attend(1, 1)
    share_sums(1)
    own_a = merge(0)
    own_b = merge(1)
    own_a.wait()
    own_b.wait()
    aout_copy.wait()
    for copy in gathers[0] + gathers[1]:
        copy.wait_recv()
    for copy in gathers[0] + gathers[1] + sends[0] + sends[1] + fwds:
        copy.wait_send()

    for f, col in enumerate(FEATURES):
        seven = kt.at[pl.ds(0, 7 * PIECE), pl.ds(col, 256)]
        send(seven, seven, xsem.at[f], xrsem.at[f], partner, k).wait_send()

    @pl.when(p < last)
    def _():
        to_right.wait_send()
        ids_right.wait_send()
        tail_right.wait_send()

    @pl.when(p > 0)
    def _():
        to_left.wait_send()


def body(
    atoms,
    atom_gain,
    atom_qkv,
    atom_proj,
    atom_bias,
    window_shift,
    token_of_atom,
    agg_weight,
    token_gain,
    token_q,
    token_kv,
    token_o,
    pair_bias,
):
    hbm = pl.BlockSpec(memory_space=pl.ANY)
    vm = pltpu.VMEM
    dma = pltpu.SemaphoreType.DMA
    return pl.pallas_call(
        kernel,
        out_shape=(
            jax.ShapeDtypeStruct((AR, 128), BF16),
            jax.ShapeDtypeStruct((TR, CT), BF16),
        ),
        in_specs=[pl.BlockSpec(memory_space=pltpu.SMEM)] + [hbm] * 12,
        out_specs=(hbm, hbm),
        scratch_shapes=[
            vm((EXT, 128), BF16),
            vm((1, 128), F32),
            vm((128, 384), BF16),
            vm((128, 128), BF16),
            vm((4, AR, WK), BF16),
            vm((1, AR + TAIL), I32),
            vm((128, CT), BF16),
            vm((CT,), F32),
            vm((CT, CT), BF16),
            vm((CT, 2 * CT), BF16),
            vm((CT, CT), BF16),
            vm((TH, TR, 2 * TR), BF16),
            vm((AR, 128), BF16),
            vm((EXT, 128), F32),
            vm((EXT, 128), F32),
            vm((AR, 128), BF16),
            vm((AR + TAIL, 128), BF16),
            vm((TR, AR + TAIL), BF16),
            vm((3, AR + TAIL, 256), BF16),
            vm((TR, CT), BF16),
            vm((TR, CT), BF16),
            vm((TR, CT), BF16),
            vm((TR, CT), BF16),
            vm((2 * TR, CT), BF16),
            vm((2 * TR, CT), BF16),
            vm((2 * TR, CT), BF16),
            vm((TR, CT), F32),
            vm((TR, 128), F32),
            vm((TR, CT), BF16),
            vm((8, 32, CT), BF16),
            vm((8, 16, CT), BF16),
            vm((8, 8, 128), F32),
            vm((8, 8, 128), F32),
            vm((8, 8, 128), F32),
            vm((8, 8, 128), F32),
            vm((32, CT), BF16),
            vm((16, CT), BF16),
            dma((11,)),
            dma,
            dma((3,)),
            dma((4,)),
            dma((4,)),
            dma((3,)),
            dma((3,)),
            dma((3,)),
            dma((3,)),
            dma((2, 4)),
            dma((2, 4)),
            dma((2,)),
            dma((2,)),
        ],
        compiler_params=pltpu.CompilerParams(
            collective_id=0, has_side_effects=True, vmem_limit_bytes=60 * 1024 * 1024
        ),
    )(
        window_shift,
        atoms,
        atom_gain.reshape(1, 128),
        atom_qkv,
        atom_proj,
        atom_bias,
        token_of_atom.reshape(1, AR),
        agg_weight,
        token_gain,
        token_q,
        token_kv,
        token_o,
        pair_bias,
    )


def solution(mesh):
    return jax.shard_map(
        body,
        mesh=mesh,
        in_specs=(
            P("pb", None),
            P(),
            P(),
            P(),
            P(None, "pb", None),
            P("pb"),
            P("pb"),
            P(),
            P(),
            P(),
            P(),
            P(),
            P(None, "pb", "ka"),
        ),
        out_specs=(P("pb", None), P("pb", None)),
        check_vma=False,
    )
```

```python
import functools
import math

import jax
import jax.numpy as jnp
from jax import lax
from jax.experimental import pallas as pl
from jax.experimental.pallas import tpu as pltpu
from jax.sharding import PartitionSpec as P

F32, BF16, I32 = jnp.float32, jnp.bfloat16, jnp.int32
AR, HALO, TAIL, WQ, WK = 3072, 64, 384, 32, 128
EXT = AR + 2 * HALO
TR, CT, TH, HD = 384, 768, 16, 48
PIECE = TR // 8
PARTS = ((0, 256), (256, 128))
WINDOWS = AR // WQ
UNROLL = 8
CHUNKS = (((0, 8, 0, 384), (8, 14, 384, 256), (14, 16, 640, 128)), ((0, 8, 0, 384), (8, 16, 384, 384)))
FEATURES = (0, 256, 512)
NT = (((1,), (1,)), ((), ()))
NN = (((1,), (0,)), ((), ()))


def iota(shape, dim):
    return lax.broadcasted_iota(I32, shape, dim)


def mm(a, b, dims=NN):
    return lax.dot_general(a, b, dims, preferred_element_type=F32)


def normed(x, gain):
    centre = jnp.mean(x, axis=-1, keepdims=True)
    diff = x - centre
    spread = jnp.mean(diff * diff, axis=-1, keepdims=True)
    return (diff * lax.rsqrt(spread + 1e-05) * gain).astype(BF16)


def kernel(
    shift_ref,
    atoms_h,
    again_h,
    qkv_h,
    proj_h,
    abias_h,
    ids_h,
    agg_h,
    tgain_h,
    wq_h,
    wkv_h,
    wo_h,
    pair_h,
    aout_h,
    tout_h,
    xs,
    again,
    wqkv,
    wproj,
    ab,
    ids,
    wagg,
    tgain,
    wq,
    wkv,
    wo,
    pbm,
    qs,
    kf,
    vf,
    ms,
    ao,
    hot,
    hid,
    rly,
    kn,
    rep,
    nrm,
    qt,
    kt,
    kk,
    vv,
    osc,
    mlb,
    mixb,
    rbuf_a,
    rbuf_b,
    mlp_a,
    mlp_b,
    rml_a,
    rml_b,
    obuf_a,
    obuf_b,
    lsem,
    psem,
    osem,
    hs,
    hr,
    xsem,
    xrsem,
    rls,
    rlr,
    rfs,
    fs,
    fr,
    rs,
    rr,
    gs,
    gr,
):
    rbuf, mlp, rml, obuf = (rbuf_a, rbuf_b), (mlp_a, mlp_b), (rml_a, rml_b), (obuf_a, obuf_b)
    p = lax.axis_index("pb")
    k = lax.axis_index("ka")
    c = lax.rem(p, 2)
    cp = lax.div(p, 2)
    zh, zl = lax.rem(cp, 2), lax.rem(k, 2)
    outer = zh == zl
    cp_flip, k_flip, p_flip = cp + 1 - 2 * zh, k + 1 - 2 * zl, p + 2 - 4 * zh
    last = 15
    barrier = pltpu.get_barrier_semaphore()

    def dev(pb, ka):
        return {"pb": pb, "ka": ka}

    def hello(pb, ka):
        pl.semaphore_signal(barrier, inc=1, device_id=dev(pb, ka), device_id_type=pl.DeviceIdType.MESH)

    def send(src, dst, ssem, rsem, pb, ka):
        return pltpu.make_async_remote_copy(
            src_ref=src,
            dst_ref=dst,
            send_sem=ssem,
            recv_sem=rsem,
            device_id=dev(pb, ka),
            device_id_type=pl.DeviceIdType.MESH,
        )

    copies = {}

    def load(name, src, dst, sem):
        copies[name] = pltpu.make_async_copy(src, dst, sem)
        copies[name].start()

    load("atoms", atoms_h, xs.at[pl.ds(HALO, AR)], lsem.at[0])
    load("again", again_h, again, lsem.at[1])
    load("qkv", qkv_h, wqkv, lsem.at[2])
    @pl.when(p > 0)
    def _():
        hello(p - 1, k)

    @pl.when(p < last)
    def _():
        hello(p + 1, k)

    def direct(i):
        return lax.rem(cp + i, 8) * 2 + c

    def relayed(x):
        return (2 * x + zh) * 2 + c

    for i in range(1, 8):
        hello(p, lax.rem(k + i, 8))

    @pl.when(outer)
    def _():
        for i in (2, 4, 6):
            hello(direct(i), cp)
        for x in range(4):
            hello(relayed(x), cp_flip)
        hello(p_flip, k_flip)

    @pl.when(jnp.logical_not(outer))
    def _():
        for i in range(1, 8):
            hello(direct(i), cp)
        for y in range(4):
            hello(2 * k_flip + c, 2 * y + 1 - zl)
            hello(2 * k + c, 2 * y + 1 - zl)

    @pl.when(jnp.logical_and(outer, k != cp))
    def _():
        for s in range(8):
            hello(2 * k + c, s)

    load("abias", abias_h, ab, lsem.at[3])
    load("proj", proj_h, wproj, lsem.at[4])
    load("agg", agg_h, wagg, lsem.at[5])
    load("ids", ids_h, ids.at[:, pl.ds(0, AR)], lsem.at[6])
    load("tgain", tgain_h, tgain, lsem.at[7])
    load("wq", wq_h, wq, lsem.at[8])
    load("wkv", wkv_h, wkv, lsem.at[9])
    load("wo", wo_h, wo, lsem.at[10])
    load("pair", pair_h, pbm, psem)

    scale = 1.0 / math.sqrt(32.0)

    def project(parts, rows, queries):
        outs = [
            mm(normed(xs[pl.ds(row, rows), :].astype(F32), again[...]), wqkv[...]) for row in parts
        ]
        for row, y in zip(parts, outs):
            if queries:
                qs[pl.ds(row - HALO, rows), :] = (y[:, 0:128] * scale).astype(BF16)
            kf[pl.ds(row, rows), :] = y[:, 128:256].astype(BF16).astype(F32)
            vf[pl.ds(row, rows), :] = y[:, 256:384].astype(BF16).astype(F32)

    copies["atoms"].wait()
    copies["again"].wait()
    copies["qkv"].wait()

    def project_own(i, carry):
        base = HALO + i * 768
        project([pl.multiple_of(base + u * 256, 64) for u in range(3)], 256, True)
        return carry

    lax.fori_loop(0, AR // 768, project_own, 0)

    copies["abias"].wait()
    copies["proj"].wait()

    head_mask = jnp.where(
        (iota((128, 128), 0) >> 5) == (iota((128, 128), 1) >> 5), 1.0, 0.0
    ).astype(BF16)
    lane_head = iota((WQ, 128), 1) >> 5
    ones = jnp.ones((WK, 128), BF16)

    def by_head(o):
        return jnp.where(
            lane_head == 0,
            o[0:32],
            jnp.where(lane_head == 1, o[32:64], jnp.where(lane_head == 2, o[64:96], o[96:128])),
        )

    def scores(b, masked):
        base = pl.multiple_of(b * WQ, WQ)
        first = base + jnp.clip(shift_ref[b], -HALO, WQ - HALO)
        kw = kf[pl.ds(first + HALO, WK), :].astype(BF16)
        q = qs[pl.ds(base, WQ), :]
        q4 = jnp.concatenate([q, q, q, q], axis=0) * head_mask
        s = mm(q4, kw, NT) + ab[:, pl.ds(base, WQ), :].reshape(128, WK).astype(F32)
        if masked:
            j = first + p * AR + iota((1, WK), 1)
            s = jnp.where((j >= 0) & (j < AR * 16), s, -1e30)
        return base, first, s

    def windows(lo, hi, masked):
        def group(g, carry):
            part = [scores(g * UNROLL + u, masked) for u in range(UNROLL)]
            tops = [jnp.max(s, axis=-1, keepdims=True) for _, _, s in part]
            weights = [jnp.exp(s - t).astype(BF16) for (_, _, s), t in zip(part, tops)]
            mixes = []
            for (_, first, _), w in zip(part, weights):
                vw = vf[pl.ds(first + HALO, WK), :].astype(BF16)
                mixes.append(mm(w, jnp.concatenate([vw, ones], axis=1)))
            for (base, _, _), o in zip(part, mixes):
                ms[pl.ds(base, WQ), :] = (
                    by_head(o[:, 0:128]) / by_head(o[:, 128:256])
                ).astype(BF16)
            return carry

        lax.fori_loop(lo // UNROLL, hi // UNROLL, group, 0)

    def finish_rows(row, rows):
        r = pl.ds(row, rows)
        y = xs[pl.ds(row + HALO, rows), :].astype(F32) + mm(ms[r, :], wproj[...])
        ao[r, :] = y.astype(BF16)

    def chunk(i):
        return i * 384 if isinstance(i, int) else pl.multiple_of(i * 384, 384)

    def hidden(f, parts):
        cols = pl.ds(FEATURES[f], 256)
        rows = [pl.ds(chunk(i), 384) for i in parts]
        outs = [mm(ao[r, :], wagg[:, cols]) for r in rows]
        for r, v in zip(rows, outs):
            hid[f, r, :] = (0.5 * v * (1.0 + jnp.tanh(0.5 * v))).astype(BF16)

    def hidden_three(f, lo, hi):
        def body(g, carry):
            hidden(f, [g * 3 + u for u in range(3)])
            return carry

        lax.fori_loop(lo, hi, body, 0)

    def finish(i, carry):
        finish_rows(chunk(i), 384)
        return carry

    def slots(row, rows):
        local = ids[:, pl.ds(row, rows)] - p * TR
        hits = jnp.where(local == iota((TR, rows), 0), 1.0, 0.0)
        hot[:, pl.ds(row, rows)] = hits.astype(BF16)
        mlb[...] += hits[:, 0:128] + hits[:, 128:256] + hits[:, 256:384]

    def slots_own(i, carry):
        slots(pl.multiple_of(i * 384, 128), 384)
        return carry

    windows(8, 16, False)

    greeted = (
        14
        + jnp.where(p > 0, 1, 0)
        + jnp.where(p < last, 1, 0)
        + jnp.where(k != cp, 8, 0)
        + jnp.where(outer, 1, 0)
    )
    pl.semaphore_wait(barrier, greeted)
    right = jnp.minimum(p + 1, last)
    left = jnp.maximum(p - 1, 0)
    to_right = send(
        atoms_h.at[pl.ds(AR - HALO, HALO)], xs.at[pl.ds(0, HALO)], hs.at[0], hr.at[0], right, k
    )
    to_left = send(
        atoms_h.at[pl.ds(0, HALO)], xs.at[pl.ds(HALO + AR, HALO)], hs.at[1], hr.at[1], left, k
    )
    ids_right = send(
        ids_h.at[:, pl.ds(AR - TAIL, TAIL)], ids.at[:, pl.ds(AR, TAIL)], hs.at[2], hr.at[2], right, k
    )
    tail_right = send(
        ao.at[pl.ds(AR - TAIL, TAIL)], ao.at[pl.ds(AR, TAIL)], hs.at[3], hr.at[3], right, k
    )

    @pl.when(p < last)
    def _():
        to_right.start()
        ids_right.start()

    @pl.when(p > 0)
    def _():
        to_left.start()

    windows(16, 80, False)
    copies["ids"].wait()
    mlb[...] = jnp.zeros((TR, 128), F32)
    lax.fori_loop(0, AR // 384, slots_own, 0)

    @pl.when(p > 0)
    def _():
        to_right.wait_recv()

    @pl.when(p < last)
    def _():
        to_left.wait_recv()

    @pl.when(p == 0)
    def _():
        xs[pl.ds(0, HALO), :] = jnp.zeros((HALO, 128), BF16)

    @pl.when(p == last)
    def _():
        xs[pl.ds(HALO + AR, HALO), :] = jnp.zeros((HALO, 128), BF16)

    project([0, HALO + AR], HALO, False)
    windows(80, 96, True)
    finish_rows(AR - TAIL, TAIL)

    @pl.when(p < last)
    def _():
        tail_right.start()

    lax.fori_loop(1, 6, finish, 0)
    copies["agg"].wait()
    hidden(0, (1, 2, 3))
    hidden(0, (4, 5))
    windows(0, 8, True)

    finish(0, 0)
    finish(6, 0)
    aout_copy = pltpu.make_async_copy(ao.at[pl.ds(0, AR)], aout_h, osem.at[0])
    aout_copy.start()

    copies["tgain"].wait()
    def tail_rows():
        @pl.when(p > 0)
        def _():
            ids_right.wait_recv()
            tail_right.wait_recv()

        @pl.when(p == 0)
        def _():
            ids[:, pl.ds(AR, TAIL)] = jnp.full((1, TAIL), -1, I32)
            ao[pl.ds(AR, TAIL), :] = jnp.zeros((TAIL, 128), BF16)

        slots(AR, TAIL)

    def rows48(i):
        return pl.ds(pl.multiple_of(i * PIECE, 16), PIECE)

    def landing(core, source):
        return pl.ds(pl.multiple_of(core * TR + source * PIECE, 16), PIECE)

    def half(i):
        return pl.ds(pl.multiple_of(i * TR, 16), TR)

    def pooled_sends(f):
        cols = pl.ds(FEATURES[f], 256)

        def go(i):
            send(
                rep.at[rows48(k), cols],
                kt.at[landing(c, k), cols],
                xsem.at[f],
                xrsem.at[f],
                direct(i),
                cp,
            ).start()

        @pl.when(outer)
        def _():
            hop(f).start()
            for i in (2, 4, 6):
                go(i)

        @pl.when(jnp.logical_not(outer))
        def _():
            for i in (1, 3, 5, 7, 2, 4, 6):
                go(i)

    def hop(f):
        cols = pl.ds(FEATURES[f], 256)
        return send(
            rep.at[rows48(k), cols], rly.at[:, cols], rls.at[f], rlr.at[f], p_flip, k_flip
        )

    def pass_on(f):
        cols = pl.ds(FEATURES[f], 256)

        @pl.when(outer)
        def _():
            hop(f).wait_recv()
            for x in range(4):
                send(
                    rly.at[:, cols],
                    kt.at[landing(c, k_flip), cols],
                    rfs.at[f],
                    xrsem.at[f],
                    relayed(x),
                    cp_flip,
                ).start()

    for f, col in enumerate(FEATURES):
        cols = pl.ds(col, 256)

        if f == 0:
            hidden(0, (0, 6, 7))
            pooled = mm(hot[:, 0:AR], hid[0, 0:AR, :])
            hidden(1, (0, 1, 2))
            tail_rows()
            hidden(0, (8,))
            counts = jnp.sum(mlb[...], axis=1, keepdims=True)
            pooled += mm(hot[:, AR : AR + TAIL], hid[0, AR : AR + TAIL, :])
        else:
            hidden_three(f, 2 - f, 3)
            pooled = mm(hot[...], hid[f])
        rep[:, cols] = (pooled / counts).astype(BF16)

        pooled_sends(f)

    tscale = 1.0 / math.sqrt(float(HD))
    copies["wq"].wait()
    nrm[...] = normed(rep[...].astype(F32), tgain[...].reshape(1, CT))
    pass_on(0)
    pass_on(1)
    qt[...] = (mm(nrm[...], wq[...]) * tscale).astype(BF16)
    pass_on(2)
    partner = p + 1 - 2 * c

    @pl.when(k == cp)
    def _():
        kt[half(c), :] = rep[...]

    fwds, backs = [], []
    for f, col in enumerate(FEATURES):
        cols = pl.ds(col, 256)
        fwds.append(
            send(kt.at[half(c), cols], kt.at[half(c), cols], fs.at[f], fr.at[f], partner, k)
        )
        backs.append(
            send(kt.at[half(c), cols], kt.at[half(1 - c), cols], fs.at[f], fr.at[f], partner, k)
        )

        @pl.when(k != cp)
        def _():
            send(
                kt.at[half(c), cols], kt.at[half(c), cols], xsem.at[f], xrsem.at[f], partner, k
            ).wait_recv()

        fwds[f].start()

    def project_half(i):
        r = half(i)
        kn[...] = normed(kt[r, :].astype(F32), tgain[...].reshape(1, CT))

        def keyvals(j, carry):
            cols = pl.ds(pl.multiple_of(j * 256, 256), 256)
            kk[r, cols] = mm(kn[...], wkv[:, cols]).astype(BF16)
            vcols = pl.ds(pl.multiple_of(j * 256 + CT, 256), 256)
            vv[r, cols] = mm(kn[...], wkv[:, vcols]).astype(BF16)
            return carry

        lax.fori_loop(0, CT // 256, keyvals, 0)

    copies["wkv"].wait()
    project_half(c)
    for copy in backs:
        copy.wait_recv()
    project_half(1 - c)
    copies["pair"].wait()
    rb = 128
    l128 = iota((rb, 128), 1)
    copies["wo"].wait()

    def make_heads(row, rows, together):
        def heads(group, carry):
            work = []
            for u in range(together):
                h = group * together + u
                lane0 = pl.multiple_of(jnp.minimum(lax.div(h * HD, 128), 4) * 128, 128)
                off = h * HD - lane0
                lanes = pl.ds(lane0, 256)
                lane = iota((1, 256), 1)
                mask = (lane >= off) & (lane < off + HD)
                keep = jnp.where(mask, 1.0, 0.0).astype(BF16)
                values = vv[:, lanes] * keep + (1.0 - keep)
                for r in range(row, row + rows, rb):
                    work.append((h, lanes, mask, keep, values, pl.ds(r, rb)))

            def score(h, lanes, mask, keep, values, r):
                return mm(qt[r, lanes] * keep, kk[:, lanes], NT) + pbm[h, r, :].astype(F32)

            def store(h, lanes, mask, r, top, o):
                osc[r, lanes] = jnp.where(mask, o, osc[r, lanes])
                total = jnp.where(mask[:, 0:128], o[:, 128:256], o[:, 0:128])
                mlb[r, :] = jnp.where(l128 == h, top, jnp.where(l128 == h + TH, total, mlb[r, :]))

            ahead = score(*work[0])
            done = None
            for n, (h, lanes, mask, keep, values, r) in enumerate(work):
                s = ahead
                if n + 1 < len(work):
                    ahead = score(*work[n + 1])
                top = jnp.max(s, axis=-1, keepdims=True)
                o = mm(jnp.exp(s - top).astype(BF16), values)
                if done is not None:
                    store(*done)
                done = (h, lanes, mask, r, top, o)
            store(*done)
            return carry

        return heads

    i0, j0 = iota((128, CT), 0) * HD, iota((128, CT), 1)
    expand = jnp.where((j0 >= i0) & (j0 < i0 + HD), 1.0, 0.0).astype(BF16)
    sends, gathers = ([], []), ([], [])

    def owned(part, owner):
        row, rows = PARTS[part]
        return pl.ds(pl.multiple_of(row + owner * (rows // 8), 16), rows // 8)

    def attend(part, n):
        row, rows = PARTS[part]
        lo, hi, col, width = CHUNKS[part][n]
        together = 512 // rows
        lax.fori_loop(lo // together, hi // together, make_heads(row, rows, together), 0)
        cols = pl.ds(col, width)
        mixb[pl.ds(row, rows), cols] = osc[pl.ds(row, rows), cols].astype(BF16)
        for i in range(1, 8):
            peer = lax.rem(k + i, 8)
            copy = send(
                mixb.at[owned(part, peer), cols],
                rbuf[part].at[i, :, cols],
                rs.at[part, n],
                rr.at[part, n],
                p,
                peer,
            )
            copy.start()
        every = rbuf[part].at[pl.ds(1, 7), :, cols]
        sends[part].append(send(every, every, rs.at[part, n], rr.at[part, n], p, lax.rem(k + 1, 8)))

    def share_sums(part):
        row, rows = PARTS[part]
        count = rows // 64
        grouped = mlb[pl.ds(row, rows), :].reshape(8, count, 8, 128)
        lane = iota((8, 8, 128), 2)
        packed = grouped[:, 0]
        for j in range(1, count):
            turned = pltpu.roll(grouped[:, j].reshape(64, 128), 32 * j, 1).reshape(8, 8, 128)
            packed = jnp.where(lane >= 32 * j, turned, packed)
        mlp[part][...] = packed
        for i in range(1, 8):
            peer = lax.rem(k + i, 8)
            copy = send(
                mlp[part].at[peer], rml[part].at[i], rs.at[part, 3], rr.at[part, 3], p, peer
            )
            copy.start()
        every = rml[part].at[pl.ds(1, 7)]
        sends[part].append(send(every, every, rs.at[part, 3], rr.at[part, 3], p, lax.rem(k + 1, 8)))

    def merge(part):
        row, rows = PARTS[part]
        piece, count = rows // 8, rows // 64
        rbuf[part][0, :, :] = mixb[owned(part, k), :]
        rml[part][0, :, :] = mlp[part][k, :, :]
        for copy in sends[part]:
            copy.wait_recv()
        packed = rml[part][...].reshape(64, 128)
        tops, tots = [], []
        for j in range(count):
            tops.append(packed if j == 0 else pltpu.roll(packed, 128 - 32 * j, 1))
            tots.append(pltpu.roll(packed, 128 - 32 * j - TH, 1))
        ml = jnp.stack([t.reshape(8, 8, 128) for t in tops], axis=1).reshape(8, piece, 128)
        tot = jnp.stack([t.reshape(8, 8, 128) for t in tots], axis=1).reshape(8, piece, 128)
        real = iota((8, piece, 128), 2) < TH
        ml = jnp.where(real, ml, 0.0)
        tot = jnp.where(real, tot, 1.0)
        top = jnp.max(ml, axis=0, keepdims=True)
        factor = jnp.exp(ml - top)
        weight = factor / jnp.sum(factor * tot, axis=0, keepdims=True)
        weight = weight.reshape(8 * piece, 128)
        high = weight.astype(BF16)
        low = (weight - high.astype(F32)).astype(BF16)
        wide = (mm(high, expand) + mm(low, expand)).reshape(8, piece, CT)
        mix = jnp.sum(wide * rbuf[part][...].astype(F32), axis=0).astype(BF16)
        obuf[part][...] = (rep[owned(part, k), :].astype(F32) + mm(mix, wo[...])).astype(BF16)
        own = pltpu.make_async_copy(obuf[part], tout_h.at[owned(part, k)], osem.at[1 + part])
        own.start()
        for i in range(1, 8):
            peer = lax.rem(k + i, 8)
            copy = send(
                obuf[part], tout_h.at[owned(part, k)], gs.at[part], gr.at[part], p, peer
            )
            copy.start()
        every = tout_h.at[pl.ds(row, 7 * piece)]
        gathers[part].append(send(every, every, gs.at[part], gr.at[part], p, lax.rem(k + 1, 8)))
        return own

    for n in range(len(CHUNKS[0])):
        attend(0, n)
    share_sums(0)
    attend(1, 0)
    attend(1, 1)
    share_sums(1)
    own_a = merge(0)
    own_b = merge(1)
    own_a.wait()
    own_b.wait()
    aout_copy.wait()
    for copy in gathers[0] + gathers[1]:
        copy.wait_recv()
    for copy in gathers[0] + gathers[1] + sends[0] + sends[1] + fwds:
        copy.wait_send()

    for f, col in enumerate(FEATURES):
        cols = pl.ds(col, 256)

        def sent(count, sem):
            some = kt.at[pl.ds(0, count * PIECE), cols]
            send(some, some, sem, xrsem.at[f], partner, k).wait_send()

        @pl.when(outer)
        def _():
            hop(f).wait_send()
            sent(3, xsem.at[f])
            sent(4, rfs.at[f])

        @pl.when(jnp.logical_not(outer))
        def _():
            sent(7, xsem.at[f])

    @pl.when(p < last)
    def _():
        to_right.wait_send()
        ids_right.wait_send()
        tail_right.wait_send()

    @pl.when(p > 0)
    def _():
        to_left.wait_send()


def body(
    atoms,
    atom_gain,
    atom_qkv,
    atom_proj,
    atom_bias,
    window_shift,
    token_of_atom,
    agg_weight,
    token_gain,
    token_q,
    token_kv,
    token_o,
    pair_bias,
):
    hbm = pl.BlockSpec(memory_space=pl.ANY)
    vm = pltpu.VMEM
    dma = pltpu.SemaphoreType.DMA
    return pl.pallas_call(
        kernel,
        out_shape=(
            jax.ShapeDtypeStruct((AR, 128), BF16),
            jax.ShapeDtypeStruct((TR, CT), BF16),
        ),
        in_specs=[pl.BlockSpec(memory_space=pltpu.SMEM)] + [hbm] * 12,
        out_specs=(hbm, hbm),
        scratch_shapes=[
            vm((EXT, 128), BF16),
            vm((1, 128), F32),
            vm((128, 384), BF16),
            vm((128, 128), BF16),
            vm((4, AR, WK), BF16),
            vm((1, AR + TAIL), I32),
            vm((128, CT), BF16),
            vm((CT,), F32),
            vm((CT, CT), BF16),
            vm((CT, 2 * CT), BF16),
            vm((CT, CT), BF16),
            vm((TH, TR, 2 * TR), BF16),
            vm((AR, 128), BF16),
            vm((EXT, 128), F32),
            vm((EXT, 128), F32),
            vm((AR, 128), BF16),
            vm((AR + TAIL, 128), BF16),
            vm((TR, AR + TAIL), BF16),
            vm((3, AR + TAIL, 256), BF16),
            vm((PIECE, CT), BF16),
            vm((TR, CT), BF16),
            vm((TR, CT), BF16),
            vm((TR, CT), BF16),
            vm((TR, CT), BF16),
            vm((2 * TR, CT), BF16),
            vm((2 * TR, CT), BF16),
            vm((2 * TR, CT), BF16),
            vm((TR, CT), F32),
            vm((TR, 128), F32),
            vm((TR, CT), BF16),
            vm((8, 32, CT), BF16),
            vm((8, 16, CT), BF16),
            vm((8, 8, 128), F32),
            vm((8, 8, 128), F32),
            vm((8, 8, 128), F32),
            vm((8, 8, 128), F32),
            vm((32, CT), BF16),
            vm((16, CT), BF16),
            dma((11,)),
            dma,
            dma((3,)),
            dma((4,)),
            dma((4,)),
            dma((3,)),
            dma((3,)),
            dma((3,)),
            dma((3,)),
            dma((3,)),
            dma((3,)),
            dma((3,)),
            dma((2, 4)),
            dma((2, 4)),
            dma((2,)),
            dma((2,)),
        ],
        compiler_params=pltpu.CompilerParams(
            collective_id=0, has_side_effects=True, vmem_limit_bytes=60 * 1024 * 1024
        ),
    )(
        window_shift,
        atoms,
        atom_gain.reshape(1, 128),
        atom_qkv,
        atom_proj,
        atom_bias,
        token_of_atom.reshape(1, AR),
        agg_weight,
        token_gain,
        token_q,
        token_kv,
        token_o,
        pair_bias,
    )


def solution(mesh):
    return jax.shard_map(
        body,
        mesh=mesh,
        in_specs=(
            P("pb", None),
            P(),
            P(),
            P(),
            P(None, "pb", None),
            P("pb"),
            P("pb"),
            P(),
            P(),
            P(),
            P(),
            P(),
            P(None, "pb", "ka"),
        ),
        out_specs=(P("pb", None), P("pb", None)),
        check_vma=False,
    )
```

```python
import functools
import math

import jax
import jax.numpy as jnp
from jax import lax
from jax.experimental import pallas as pl
from jax.experimental.pallas import tpu as pltpu
from jax.sharding import PartitionSpec as P

F32, BF16, I32 = jnp.float32, jnp.bfloat16, jnp.int32
AR, HALO, TAIL, WQ, WK = 3072, 64, 384, 32, 128
EXT = AR + 2 * HALO
TR, CT, TH, HD = 384, 768, 16, 48
PIECE = TR // 8
PARTS = ((0, 256), (256, 128))
WINDOWS = AR // WQ
UNROLL = 8
CHUNKS = (((0, 8, 0, 384), (8, 14, 384, 256), (14, 16, 640, 128)), ((0, 8, 0, 384), (8, 16, 384, 384)))
FEATURES = (0, 256, 512)
NT = (((1,), (1,)), ((), ()))
NN = (((1,), (0,)), ((), ()))


def iota(shape, dim):
    return lax.broadcasted_iota(I32, shape, dim)


def mm(a, b, dims=NN):
    return lax.dot_general(a, b, dims, preferred_element_type=F32)


def normed(x, gain):
    centre = jnp.mean(x, axis=-1, keepdims=True)
    diff = x - centre
    spread = jnp.mean(diff * diff, axis=-1, keepdims=True)
    return (diff * lax.rsqrt(spread + 1e-05) * gain).astype(BF16)


def kernel(
    shift_ref,
    atoms_h,
    again_h,
    qkv_h,
    proj_h,
    abias_h,
    ids_h,
    agg_h,
    tgain_h,
    wq_h,
    wkv_h,
    wo_h,
    pair_h,
    aout_h,
    tout_h,
    xs,
    again,
    wqkv,
    wproj,
    ab,
    ids,
    wagg,
    tgain,
    wq,
    wkv,
    wo,
    pbm,
    qs,
    kf,
    vf,
    ms,
    ao,
    hot,
    hid,
    rly,
    kn,
    rep,
    nrm,
    qt,
    kt,
    kk,
    vv,
    osc,
    mlb,
    mixb,
    rbuf_a,
    rbuf_b,
    mlp_a,
    mlp_b,
    rml_a,
    rml_b,
    obuf_a,
    obuf_b,
    lsem,
    psem,
    osem,
    hs,
    hr,
    xsem,
    xrsem,
    rls,
    rlr,
    rfs,
    fs,
    fr,
    rs,
    rr,
    gs,
    gr,
):
    rbuf, mlp, rml, obuf = (rbuf_a, rbuf_b), (mlp_a, mlp_b), (rml_a, rml_b), (obuf_a, obuf_b)
    p = lax.axis_index("pb")
    k = lax.axis_index("ka")
    c = lax.rem(p, 2)
    cp = lax.div(p, 2)
    zh, zl = lax.rem(cp, 2), lax.rem(k, 2)
    outer = zh == zl
    cp_flip, k_flip, p_flip = cp + 1 - 2 * zh, k + 1 - 2 * zl, p + 2 - 4 * zh
    last = 15
    barrier = pltpu.get_barrier_semaphore()

    def dev(pb, ka):
        return {"pb": pb, "ka": ka}

    def hello(pb, ka):
        pl.semaphore_signal(barrier, inc=1, device_id=dev(pb, ka), device_id_type=pl.DeviceIdType.MESH)

    def send(src, dst, ssem, rsem, pb, ka):
        return pltpu.make_async_remote_copy(
            src_ref=src,
            dst_ref=dst,
            send_sem=ssem,
            recv_sem=rsem,
            device_id=dev(pb, ka),
            device_id_type=pl.DeviceIdType.MESH,
        )

    copies = {}

    def load(name, src, dst, sem):
        copies[name] = pltpu.make_async_copy(src, dst, sem)
        copies[name].start()

    load("atoms", atoms_h, xs.at[pl.ds(HALO, AR)], lsem.at[0])
    load("again", again_h, again, lsem.at[1])
    load("qkv", qkv_h, wqkv, lsem.at[2])
    @pl.when(p > 0)
    def _():
        hello(p - 1, k)

    @pl.when(p < last)
    def _():
        hello(p + 1, k)

    def direct(i):
        return lax.rem(cp + i, 8) * 2 + c

    def relayed(x):
        return (2 * x + zh) * 2 + c

    for i in range(1, 8):
        hello(p, lax.rem(k + i, 8))

    @pl.when(outer)
    def _():
        for i in (2, 4, 6):
            hello(direct(i), cp)
        for x in range(4):
            hello(relayed(x), cp_flip)
        hello(p_flip, k_flip)

    @pl.when(jnp.logical_not(outer))
    def _():
        for i in range(1, 8):
            hello(direct(i), cp)
        for y in range(4):
            hello(2 * k_flip + c, 2 * y + 1 - zl)
            hello(2 * k + c, 2 * y + 1 - zl)

    @pl.when(jnp.logical_and(outer, k != cp))
    def _():
        for s in range(8):
            hello(2 * k + c, s)

    load("abias", abias_h, ab, lsem.at[3])
    load("proj", proj_h, wproj, lsem.at[4])
    load("agg", agg_h, wagg, lsem.at[5])
    load("ids", ids_h, ids.at[:, pl.ds(0, AR)], lsem.at[6])
    load("tgain", tgain_h, tgain, lsem.at[7])
    load("wq", wq_h, wq, lsem.at[8])
    load("wkv", wkv_h, wkv, lsem.at[9])
    load("wo", wo_h, wo, lsem.at[10])
    load("pair", pair_h, pbm, psem)

    scale = 1.0 / math.sqrt(32.0)

    def project(parts, rows, queries):
        outs = [
            mm(normed(xs[pl.ds(row, rows), :].astype(F32), again[...]), wqkv[...]) for row in parts
        ]
        for row, y in zip(parts, outs):
            if queries:
                qs[pl.ds(row - HALO, rows), :] = (y[:, 0:128] * scale).astype(BF16)
            kf[pl.ds(row, rows), :] = y[:, 128:256].astype(BF16).astype(F32)
            vf[pl.ds(row, rows), :] = y[:, 256:384].astype(BF16).astype(F32)

    copies["atoms"].wait()
    copies["again"].wait()
    copies["qkv"].wait()

    def project_own(i, carry):
        base = HALO + i * 768
        project([pl.multiple_of(base + u * 256, 64) for u in range(3)], 256, True)
        return carry

    lax.fori_loop(0, AR // 768, project_own, 0)

    copies["abias"].wait()
    copies["proj"].wait()

    head_mask = jnp.where(
        (iota((128, 128), 0) >> 5) == (iota((128, 128), 1) >> 5), 1.0, 0.0
    ).astype(BF16)
    lane_head = iota((WQ, 128), 1) >> 5
    ones = jnp.ones((WK, 128), BF16)

    def by_head(o):
        return jnp.where(
            lane_head == 0,
            o[0:32],
            jnp.where(lane_head == 1, o[32:64], jnp.where(lane_head == 2, o[64:96], o[96:128])),
        )

    def scores(b, masked):
        base = pl.multiple_of(b * WQ, WQ)
        first = base + jnp.clip(shift_ref[b], -HALO, WQ - HALO)
        kw = kf[pl.ds(first + HALO, WK), :].astype(BF16)
        q = qs[pl.ds(base, WQ), :]
        q4 = jnp.concatenate([q, q, q, q], axis=0) * head_mask
        s = mm(q4, kw, NT) + ab[:, pl.ds(base, WQ), :].reshape(128, WK).astype(F32)
        if masked:
            j = first + p * AR + iota((1, WK), 1)
            s = jnp.where((j >= 0) & (j < AR * 16), s, -1e30)
        return base, first, s

    def windows(lo, hi, masked):
        def group(g, carry):
            part = [scores(g * UNROLL + u, masked) for u in range(UNROLL)]
            tops = [jnp.max(s, axis=-1, keepdims=True) for _, _, s in part]
            weights = [jnp.exp(s - t).astype(BF16) for (_, _, s), t in zip(part, tops)]
            mixes = []
            for (_, first, _), w in zip(part, weights):
                vw = vf[pl.ds(first + HALO, WK), :].astype(BF16)
                mixes.append(mm(w, jnp.concatenate([vw, ones], axis=1)))
            for (base, _, _), o in zip(part, mixes):
                ms[pl.ds(base, WQ), :] = (
                    by_head(o[:, 0:128]) / by_head(o[:, 128:256])
                ).astype(BF16)
            return carry

        lax.fori_loop(lo // UNROLL, hi // UNROLL, group, 0)

    def finish_rows(row, rows):
        r = pl.ds(row, rows)
        y = xs[pl.ds(row + HALO, rows), :].astype(F32) + mm(ms[r, :], wproj[...])
        ao[r, :] = y.astype(BF16)

    def chunk(i):
        return i * 384 if isinstance(i, int) else pl.multiple_of(i * 384, 384)

    def hidden(f, parts):
        cols = pl.ds(FEATURES[f], 256)
        rows = [pl.ds(chunk(i), 384) for i in parts]
        outs = [mm(ao[r, :], wagg[:, cols]) for r in rows]
        for r, v in zip(rows, outs):
            hid[f, r, :] = (0.5 * v * (1.0 + jnp.tanh(0.5 * v))).astype(BF16)

    def hidden_three(f, lo, hi):
        def body(g, carry):
            hidden(f, [g * 3 + u for u in range(3)])
            return carry

        lax.fori_loop(lo, hi, body, 0)

    def finish(i, carry):
        finish_rows(chunk(i), 384)
        return carry

    def slots(row, rows):
        local = ids[:, pl.ds(row, rows)] - p * TR
        hits = jnp.where(local == iota((TR, rows), 0), 1.0, 0.0)
        hot[:, pl.ds(row, rows)] = hits.astype(BF16)
        mlb[...] += hits[:, 0:128] + hits[:, 128:256] + hits[:, 256:384]

    def slots_own(i, carry):
        slots(pl.multiple_of(i * 384, 128), 384)
        return carry

    windows(8, 16, False)

    greeted = (
        14
        + jnp.where(p > 0, 1, 0)
        + jnp.where(p < last, 1, 0)
        + jnp.where(k != cp, 8, 0)
        + jnp.where(outer, 1, 0)
    )
    pl.semaphore_wait(barrier, greeted)
    right = jnp.minimum(p + 1, last)
    left = jnp.maximum(p - 1, 0)
    to_right = send(
        atoms_h.at[pl.ds(AR - HALO, HALO)], xs.at[pl.ds(0, HALO)], hs.at[0], hr.at[0], right, k
    )
    to_left = send(
        atoms_h.at[pl.ds(0, HALO)], xs.at[pl.ds(HALO + AR, HALO)], hs.at[1], hr.at[1], left, k
    )
    ids_right = send(
        ids_h.at[:, pl.ds(AR - TAIL, TAIL)], ids.at[:, pl.ds(AR, TAIL)], hs.at[2], hr.at[2], right, k
    )
    tail_right = send(
        ao.at[pl.ds(AR - TAIL, TAIL)], ao.at[pl.ds(AR, TAIL)], hs.at[3], hr.at[3], right, k
    )

    @pl.when(p < last)
    def _():
        to_right.start()
        ids_right.start()

    @pl.when(p > 0)
    def _():
        to_left.start()

    windows(16, 80, False)
    copies["ids"].wait()
    mlb[...] = jnp.zeros((TR, 128), F32)
    lax.fori_loop(0, AR // 384, slots_own, 0)

    @pl.when(p > 0)
    def _():
        to_right.wait_recv()

    @pl.when(p < last)
    def _():
        to_left.wait_recv()

    @pl.when(p == 0)
    def _():
        xs[pl.ds(0, HALO), :] = jnp.zeros((HALO, 128), BF16)

    @pl.when(p == last)
    def _():
        xs[pl.ds(HALO + AR, HALO), :] = jnp.zeros((HALO, 128), BF16)

    project([0, HALO + AR], HALO, False)
    windows(80, 96, True)
    finish_rows(AR - TAIL, TAIL)

    @pl.when(p < last)
    def _():
        tail_right.start()

    lax.fori_loop(1, 6, finish, 0)
    copies["agg"].wait()
    hidden(0, (1, 2, 3))
    hidden(0, (4, 5))
    windows(0, 8, True)

    finish(0, 0)
    finish(6, 0)
    aout_copy = pltpu.make_async_copy(ao.at[pl.ds(0, AR)], aout_h, osem.at[0])
    aout_copy.start()

    copies["tgain"].wait()
    def tail_rows():
        @pl.when(p > 0)
        def _():
            ids_right.wait_recv()
            tail_right.wait_recv()

        @pl.when(p == 0)
        def _():
            ids[:, pl.ds(AR, TAIL)] = jnp.full((1, TAIL), -1, I32)
            ao[pl.ds(AR, TAIL), :] = jnp.zeros((TAIL, 128), BF16)

        slots(AR, TAIL)

    def rows48(i):
        return pl.ds(pl.multiple_of(i * PIECE, 16), PIECE)

    def landing(core, source):
        return pl.ds(pl.multiple_of(core * TR + source * PIECE, 16), PIECE)

    def half(i):
        return pl.ds(pl.multiple_of(i * TR, 16), TR)

    def pooled_sends(f):
        cols = pl.ds(FEATURES[f], 256)

        def go(i):
            send(
                rep.at[rows48(k), cols],
                kt.at[landing(c, k), cols],
                xsem.at[f],
                xrsem.at[f],
                direct(i),
                cp,
            ).start()

        @pl.when(outer)
        def _():
            hop(f).start()
            for i in (2, 4, 6):
                go(i)

        @pl.when(jnp.logical_not(outer))
        def _():
            for i in (1, 3, 5, 7, 2, 4, 6):
                go(i)

    def hop(f):
        cols = pl.ds(FEATURES[f], 256)
        return send(
            rep.at[rows48(k), cols], rly.at[:, cols], rls.at[f], rlr.at[f], p_flip, k_flip
        )

    def pass_on(f):
        cols = pl.ds(FEATURES[f], 256)

        @pl.when(outer)
        def _():
            hop(f).wait_recv()
            for x in range(4):
                send(
                    rly.at[:, cols],
                    kt.at[landing(c, k_flip), cols],
                    rfs.at[f],
                    xrsem.at[f],
                    relayed(x),
                    cp_flip,
                ).start()

    for f, col in enumerate(FEATURES):
        cols = pl.ds(col, 256)

        if f == 0:
            hidden(0, (0, 6, 7))
            pooled = mm(hot[:, 0:AR], hid[0, 0:AR, :])
            hidden(1, (0, 1, 2))
            tail_rows()
            hidden(0, (8,))
            counts = jnp.sum(mlb[...], axis=1, keepdims=True)
            pooled += mm(hot[:, AR : AR + TAIL], hid[0, AR : AR + TAIL, :])
        else:
            hidden_three(f, 2 - f, 3)
            pooled = mm(hot[...], hid[f])
        rep[:, cols] = (pooled / counts).astype(BF16)

        pooled_sends(f)

    tscale = 1.0 / math.sqrt(float(HD))
    copies["wq"].wait()
    nrm[...] = normed(rep[...].astype(F32), tgain[...].reshape(1, CT))
    pass_on(0)
    pass_on(1)
    qt[...] = (mm(nrm[...], wq[...]) * tscale).astype(BF16)
    pass_on(2)
    partner = p + 1 - 2 * c

    @pl.when(k == cp)
    def _():
        kt[half(c), :] = rep[...]

    fwds, backs = [], []
    for f, col in enumerate(FEATURES):
        cols = pl.ds(col, 256)
        fwds.append(
            send(kt.at[half(c), cols], kt.at[half(c), cols], fs.at[f], fr.at[f], partner, k)
        )
        backs.append(
            send(kt.at[half(c), cols], kt.at[half(1 - c), cols], fs.at[f], fr.at[f], partner, k)
        )

        @pl.when(k != cp)
        def _():
            send(
                kt.at[half(c), cols], kt.at[half(c), cols], xsem.at[f], xrsem.at[f], partner, k
            ).wait_recv()

        fwds[f].start()

    def project_half(i):
        r = half(i)
        kn[...] = normed(kt[r, :].astype(F32), tgain[...].reshape(1, CT))

        def keyvals(j, carry):
            cols = pl.ds(pl.multiple_of(j * 256, 256), 256)
            kk[r, cols] = mm(kn[...], wkv[:, cols]).astype(BF16)
            vcols = pl.ds(pl.multiple_of(j * 256 + CT, 256), 256)
            vv[r, cols] = mm(kn[...], wkv[:, vcols]).astype(BF16)
            return carry

        lax.fori_loop(0, CT // 256, keyvals, 0)

    copies["wkv"].wait()
    project_half(c)
    for copy in backs:
        copy.wait_recv()
    project_half(1 - c)
    copies["pair"].wait()
    rb = 128
    l128 = iota((rb, 128), 1)
    copies["wo"].wait()

    def make_heads(row, rows, together):
        def heads(group, carry):
            work = []
            for u in range(together):
                h = group * together + u
                lane0 = pl.multiple_of(jnp.minimum(lax.div(h * HD, 128), 4) * 128, 128)
                off = h * HD - lane0
                lanes = pl.ds(lane0, 256)
                lane = iota((1, 256), 1)
                mask = (lane >= off) & (lane < off + HD)
                keep = jnp.where(mask, 1.0, 0.0).astype(BF16)
                values = vv[:, lanes] * keep + (1.0 - keep)
                for r in range(row, row + rows, rb):
                    work.append((h, lanes, mask, keep, values, pl.ds(r, rb)))

            def score(h, lanes, mask, keep, values, r):
                return mm(qt[r, lanes] * keep, kk[:, lanes], NT) + pbm[h, r, :].astype(F32)

            def store(h, lanes, mask, r, top, o):
                osc[r, lanes] = jnp.where(mask, o, osc[r, lanes])
                total = jnp.where(mask[:, 0:128], o[:, 128:256], o[:, 0:128])
                mlb[r, :] = jnp.where(l128 == h, top, jnp.where(l128 == h + TH, total, mlb[r, :]))

            ahead = score(*work[0])
            done = None
            for n, (h, lanes, mask, keep, values, r) in enumerate(work):
                s = ahead
                if n + 1 < len(work):
                    ahead = score(*work[n + 1])
                top = jnp.max(s, axis=-1, keepdims=True)
                o = mm(jnp.exp(s - top).astype(BF16), values)
                if done is not None:
                    store(*done)
                done = (h, lanes, mask, r, top, o)
            store(*done)
            return carry

        return heads

    i0, j0 = iota((128, CT), 0) * HD, iota((128, CT), 1)
    expand = jnp.where((j0 >= i0) & (j0 < i0 + HD), 1.0, 0.0).astype(BF16)
    sends, gathers = ([], []), ([], [])

    def owned(part, owner):
        row, rows = PARTS[part]
        return pl.ds(pl.multiple_of(row + owner * (rows // 8), 16), rows // 8)

    def attend(part, n):
        row, rows = PARTS[part]
        lo, hi, col, width = CHUNKS[part][n]
        together = 512 // rows
        lax.fori_loop(lo // together, hi // together, make_heads(row, rows, together), 0)
        cols = pl.ds(col, width)
        mixb[pl.ds(row, rows), cols] = osc[pl.ds(row, rows), cols].astype(BF16)
        for i in range(1, 8):
            peer = lax.rem(k + i, 8)
            copy = send(
                mixb.at[owned(part, peer), cols],
                rbuf[part].at[i, :, cols],
                rs.at[part, n],
                rr.at[part, n],
                p,
                peer,
            )
            copy.start()
        every = rbuf[part].at[pl.ds(1, 7), :, cols]
        sends[part].append(send(every, every, rs.at[part, n], rr.at[part, n], p, lax.rem(k + 1, 8)))

    def share_sums(part):
        row, rows = PARTS[part]
        count = rows // 64
        grouped = mlb[pl.ds(row, rows), :].reshape(8, count, 8, 128)
        lane = iota((8, 8, 128), 2)
        packed = grouped[:, 0]
        for j in range(1, count):
            turned = pltpu.roll(grouped[:, j].reshape(64, 128), 32 * j, 1).reshape(8, 8, 128)
            packed = jnp.where(lane >= 32 * j, turned, packed)
        mlp[part][...] = packed
        for i in range(1, 8):
            peer = lax.rem(k + i, 8)
            copy = send(
                mlp[part].at[peer], rml[part].at[i], rs.at[part, 3], rr.at[part, 3], p, peer
            )
            copy.start()
        every = rml[part].at[pl.ds(1, 7)]
        sends[part].append(send(every, every, rs.at[part, 3], rr.at[part, 3], p, lax.rem(k + 1, 8)))

    def merge(part):
        row, rows = PARTS[part]
        piece, count = rows // 8, rows // 64
        rbuf[part][0, :, :] = mixb[owned(part, k), :]
        rml[part][0, :, :] = mlp[part][k, :, :]
        for copy in sends[part]:
            copy.wait_recv()
        packed = rml[part][...].reshape(64, 128)
        tops, tots = [], []
        for j in range(count):
            tops.append(packed if j == 0 else pltpu.roll(packed, 128 - 32 * j, 1))
            tots.append(pltpu.roll(packed, 128 - 32 * j - TH, 1))
        ml = jnp.stack([t.reshape(8, 8, 128) for t in tops], axis=1).reshape(8, piece, 128)
        tot = jnp.stack([t.reshape(8, 8, 128) for t in tots], axis=1).reshape(8, piece, 128)
        real = iota((8, piece, 128), 2) < TH
        ml = jnp.where(real, ml, 0.0)
        tot = jnp.where(real, tot, 1.0)
        top = jnp.max(ml, axis=0, keepdims=True)
        factor = jnp.exp(ml - top)
        weight = factor / jnp.sum(factor * tot, axis=0, keepdims=True)
        weight = weight.reshape(8 * piece, 128)
        high = weight.astype(BF16)
        low = (weight - high.astype(F32)).astype(BF16)
        wide = (mm(high, expand) + mm(low, expand)).reshape(8, piece, CT)
        mix = jnp.sum(wide * rbuf[part][...].astype(F32), axis=0).astype(BF16)
        obuf[part][...] = (rep[owned(part, k), :].astype(F32) + mm(mix, wo[...])).astype(BF16)
        own = pltpu.make_async_copy(obuf[part], tout_h.at[owned(part, k)], osem.at[1 + part])
        own.start()
        for i in range(1, 8):
            peer = lax.rem(k + i, 8)
            copy = send(
                obuf[part], tout_h.at[owned(part, k)], gs.at[part], gr.at[part], p, peer
            )
            copy.start()
        every = tout_h.at[pl.ds(row, 7 * piece)]
        gathers[part].append(send(every, every, gs.at[part], gr.at[part], p, lax.rem(k + 1, 8)))
        return own

    for n in range(len(CHUNKS[0])):
        attend(0, n)
    share_sums(0)
    attend(1, 0)
    attend(1, 1)
    share_sums(1)
    own_a = merge(0)
    own_b = merge(1)
    own_a.wait()
    own_b.wait()
    aout_copy.wait()
    for copy in gathers[0] + gathers[1]:
        copy.wait_recv()
    for copy in gathers[0] + gathers[1] + sends[0] + sends[1] + fwds:
        copy.wait_send()

    for f, col in enumerate(FEATURES):
        cols = pl.ds(col, 256)

        def sent(count, sem):
            some = kt.at[pl.ds(0, count * PIECE), cols]
            send(some, some, sem, xrsem.at[f], partner, k).wait_send()

        @pl.when(outer)
        def _():
            hop(f).wait_send()
            sent(3, xsem.at[f])
            sent(4, rfs.at[f])

        @pl.when(jnp.logical_not(outer))
        def _():
            sent(7, xsem.at[f])

    @pl.when(p < last)
    def _():
        to_right.wait_send()
        ids_right.wait_send()
        tail_right.wait_send()

    @pl.when(p > 0)
    def _():
        to_left.wait_send()


def write_out(a_ref, t_ref, a_out, t_out, a_buf, t_buf, in_sem, out_sem):
    moves = []
    for n in range(2):
        for m, (src, buf, dst, rows) in enumerate(
            ((a_ref, a_buf, a_out, AR // 2), (t_ref, t_buf, t_out, TR // 2))
        ):
            r = pl.ds(n * rows, rows)
            moves.append(
                (
                    pltpu.make_async_copy(src.at[r], buf.at[r], in_sem.at[n, m]),
                    pltpu.make_async_copy(buf.at[r], dst.at[r], out_sem.at[n, m]),
                )
            )
    for fetch, _ in moves:
        fetch.start()
    for fetch, put in moves:
        fetch.wait()
        put.start()
    for _, put in moves:
        put.wait()


def body(
    atoms,
    atom_gain,
    atom_qkv,
    atom_proj,
    atom_bias,
    window_shift,
    token_of_atom,
    agg_weight,
    token_gain,
    token_q,
    token_kv,
    token_o,
    pair_bias,
):
    hbm = pl.BlockSpec(memory_space=pl.ANY)
    vm = pltpu.VMEM
    dma = pltpu.SemaphoreType.DMA
    shapes = (
        jax.ShapeDtypeStruct((AR, 128), BF16),
        jax.ShapeDtypeStruct((TR, CT), BF16),
    )
    aout, tout = pl.pallas_call(
        kernel,
        out_shape=shapes,
        in_specs=[pl.BlockSpec(memory_space=pltpu.SMEM)] + [hbm] * 12,
        out_specs=(hbm, hbm),
        scratch_shapes=[
            vm((EXT, 128), BF16),
            vm((1, 128), F32),
            vm((128, 384), BF16),
            vm((128, 128), BF16),
            vm((4, AR, WK), BF16),
            vm((1, AR + TAIL), I32),
            vm((128, CT), BF16),
            vm((CT,), F32),
            vm((CT, CT), BF16),
            vm((CT, 2 * CT), BF16),
            vm((CT, CT), BF16),
            vm((TH, TR, 2 * TR), BF16),
            vm((AR, 128), BF16),
            vm((EXT, 128), F32),
            vm((EXT, 128), F32),
            vm((AR, 128), BF16),
            vm((AR + TAIL, 128), BF16),
            vm((TR, AR + TAIL), BF16),
            vm((3, AR + TAIL, 256), BF16),
            vm((PIECE, CT), BF16),
            vm((TR, CT), BF16),
            vm((TR, CT), BF16),
            vm((TR, CT), BF16),
            vm((TR, CT), BF16),
            vm((2 * TR, CT), BF16),
            vm((2 * TR, CT), BF16),
            vm((2 * TR, CT), BF16),
            vm((TR, CT), F32),
            vm((TR, 128), F32),
            vm((TR, CT), BF16),
            vm((8, 32, CT), BF16),
            vm((8, 16, CT), BF16),
            vm((8, 8, 128), F32),
            vm((8, 8, 128), F32),
            vm((8, 8, 128), F32),
            vm((8, 8, 128), F32),
            vm((32, CT), BF16),
            vm((16, CT), BF16),
            dma((11,)),
            dma,
            dma((3,)),
            dma((4,)),
            dma((4,)),
            dma((3,)),
            dma((3,)),
            dma((3,)),
            dma((3,)),
            dma((3,)),
            dma((3,)),
            dma((3,)),
            dma((2, 4)),
            dma((2, 4)),
            dma((2,)),
            dma((2,)),
        ],
        compiler_params=pltpu.CompilerParams(
            collective_id=0, has_side_effects=True, vmem_limit_bytes=60 * 1024 * 1024
        ),
    )(
        window_shift,
        atoms,
        atom_gain.reshape(1, 128),
        atom_qkv,
        atom_proj,
        atom_bias,
        token_of_atom.reshape(1, AR),
        agg_weight,
        token_gain,
        token_q,
        token_kv,
        token_o,
        pair_bias,
    )
    return pl.pallas_call(
        write_out,
        out_shape=shapes,
        in_specs=[hbm, hbm],
        out_specs=(hbm, hbm),
        scratch_shapes=[vm((AR, 128), BF16), vm((TR, CT), BF16), dma((2, 2)), dma((2, 2))],
    )(aout, tout)


def solution(mesh):
    return jax.shard_map(
        body,
        mesh=mesh,
        in_specs=(
            P("pb", None),
            P(),
            P(),
            P(),
            P(None, "pb", None),
            P("pb"),
            P("pb"),
            P(),
            P(),
            P(),
            P(),
            P(),
            P(None, "pb", "ka"),
        ),
        out_specs=(P("pb", None), P("pb", None)),
        check_vma=False,
    )
```
